128 devices in a mesh: row: 8 (over y, core), col: 16 (over x, z).
Axes of the slice: x: 4, y: 4, z: 4, core: 2. Of those that a mesh axis runs over, the one named last changes fastest.
Arguments:
- points: bfloat16 [1048576, 768], P(('row', 'col')), may hold values from -6 to 6
- node_of_row: int32 [1048576], P(('row', 'col')), may hold values from 0 to 255, as said below
- init_axes: float32 [768, 8], replicated, may hold values from -0.21875 to 0.21875
Outputs:
- projected: float32 [8, 1048576], P(None, ('row', 'col'))
The draws below stay inside these ranges and needn't reach their ends.
Inputs may be any that keep to these rules, and one draw needn't show every extreme that they name: `node_of_row`: never falls along the points; every one of the 256 nodes has at least 512 points; the points of one device belong to at most 8 nodes, and exactly 8 on some device; a node may cover many devices.
All inputs are finite; a program needn't handle non-finite values.
Results may differ from the reference program's by a relative error of at most 0.0035.
The reference program's roundings to bfloat16 on the way (of `lifted`) count: a program that leaves them out, or rounds other values in their place, can miss the bound.
Values sent between devices are 32-bit elements; how exact they have to be, the bound alone decides.
A program may use at most 128 MiB of HBM per device.

```python
import jax
import jax.numpy as jnp
from jax import lax

D = 768
AXES = 8
ITERS = 3
SPAN_MOST = 8
TOK_DEV = 8192
NODES = 256
TOTAL = 1048576
GAP = 512
DEVICES = 128


def draw_node_of_row(key, part):
    key_device = jax.random.fold_in(key, 11)
    key_choose = jax.random.fold_in(key, 12)
    key_places = jax.random.fold_in(key, 13)
    key_run = jax.random.fold_in(key, 14)
    cut_slots = SPAN_MOST - 1
    slot_total = DEVICES * cut_slots
    run_length = DEVICES // 2 + 1
    run_start = jax.random.randint(key_run, (), 0, DEVICES - run_length + 1)
    pick = jax.random.randint(key_device, (), 0, DEVICES - run_length)
    favoured = jnp.where(pick < run_start, pick, pick + run_length)
    slot_index = jnp.arange(slot_total, dtype=jnp.int32)
    slot_device = slot_index // cut_slots
    scores = jax.random.permutation(key_choose, slot_total).astype(jnp.int32)
    in_run = (slot_device >= run_start) & (slot_device < run_start + run_length)
    scores = jnp.where(in_run, slot_total + 1, scores)
    scores = jnp.where(slot_device == favoured, -1 - slot_index % cut_slots, scores)
    ranked = jnp.argsort(scores, stable=True)
    chosen = jnp.zeros((slot_total,), jnp.int32).at[ranked[:NODES - 1]].set(1)
    device_keys = jax.random.split(key_places, DEVICES)
    free_range = TOK_DEV - SPAN_MOST * GAP + cut_slots
    stride = jnp.arange(cut_slots, dtype=jnp.int32) * (GAP - 1) + GAP

    def place_cuts(one_key):
        picked = jnp.sort(jax.random.permutation(one_key, free_range)[:cut_slots].astype(jnp.int32))
        return picked + stride
    places = jax.vmap(place_cuts)(device_keys)
    positions = (jnp.arange(DEVICES, dtype=jnp.int32)[:, None] * TOK_DEV + places.astype(jnp.int32)).reshape(-1)
    cuts = jnp.zeros((TOTAL,), jnp.int32).at[positions].add(chosen)
    return jnp.cumsum(cuts).astype(jnp.int32)


def block_levels(own_key, dims, cuts, least, largest):
    factor_of, own = 1.0, jax.random.fold_in(own_key, 6)
    for position, blocks in cuts:
        heights = jnp.exp(jax.random.uniform(jax.random.fold_in(own, position), (blocks,), jnp.float32, least / len(cuts), largest / len(cuts)))
        factor_of = factor_of * jnp.repeat(heights, dims[position] // blocks).reshape([-1 if axis == position else 1 for axis in range(len(dims))])
    return factor_of


def centred(stream_key, dims, scale, reach, pieces=(), kind=jnp.bfloat16):
    array = jax.random.normal(stream_key, dims, jnp.float32) * scale
    if len(pieces) > 0:
        array = block_levels(stream_key, dims, pieces, -0.22, 0.18) * array
    return jnp.clip(array, min=-reach, max=reach).astype(kind)


def setup_inputs(seed: int = 0) -> dict:
    streams_of = jax.random.split(jax.random.key(seed), 4)
    return {
        "points": centred(streams_of[0], (TOTAL, D), 1.0, 6.0, ((0, 128),)),
        "node_of_row": draw_node_of_row(jax.random.fold_in(streams_of[3], 71), 0),
        "init_axes": centred(streams_of[2], (D, AXES), D ** -0.5, 0.21875, (), jnp.float32),
    }


def orthonormal(moment):
    found = []
    for index in range(moment.shape[1]):
        vector = moment[:, index]
        for column in found:
            vector = vector - jnp.sum(column * vector) * column
        vector = vector / jnp.sqrt(jnp.sum(vector * vector))
        found.append(vector)
    return jnp.stack(found, 1)

def window_member(node_ids):
    first_node = node_ids[0]
    member = node_ids[:, None] - first_node == jnp.arange(SPAN_MOST, dtype=jnp.int32)[None, :]
    return (first_node, member.astype(jnp.float32))

def lifted_terms(block, frames, centre):
    offset = jnp.einsum('ld,ldk->lk', centre, frames, precision=lax.Precision.HIGHEST)
    flat_frames = frames.astype(jnp.bfloat16).transpose(1, 0, 2).reshape(frames.shape[1], -1)
    spread = jnp.dot(block, flat_frames, preferred_element_type=jnp.float32)
    return spread.reshape(block.shape[0], SPAN_MOST, AXES) - offset[None]

def local_moment(block, member, frames, centre):
    terms = lifted_terms(block, frames, centre)
    lifted = terms.astype(jnp.bfloat16) * member.astype(jnp.bfloat16)[:, :, None]
    moment = lax.dot_general(block, lifted.reshape(block.shape[0], -1), (((0,), (0,)), ((), ())), preferred_element_type=jnp.float32)
    moment = moment.reshape(block.shape[1], SPAN_MOST, AXES).transpose(1, 0, 2)
    column_sums = lax.optimization_barrier(jnp.sum(lifted.astype(jnp.float32), 0))
    return moment - centre[:, :, None] * column_sums[:, None, :]

def add_window(total, first_node, piece):
    current = lax.dynamic_slice_in_dim(total, first_node, SPAN_MOST, 0)
    return lax.dynamic_update_slice_in_dim(total, current + piece, first_node, 0)

def reference(points, node_of_row, init_axes):
    width = points.shape[1]
    blocks = points.reshape(DEVICES, TOK_DEV, width)
    id_blocks = node_of_row.reshape(DEVICES, TOK_DEV)
    padded = NODES + SPAN_MOST

    def mean_block(carry, item):
        node_sums, node_counts = carry
        block, node_ids = item
        first_node, member = window_member(node_ids)
        sums = lax.dot_general(member.astype(jnp.bfloat16), block, (((0,), (0,)), ((), ())), preferred_element_type=jnp.float32)
        counts = lax.optimization_barrier(jnp.sum(member, 0))
        return ((add_window(node_sums, first_node, sums), add_window(node_counts, first_node, counts)), None)
    start = (jnp.zeros((padded, width), jnp.float32), jnp.zeros((padded,), jnp.float32))
    (node_sums, node_counts), _ = lax.scan(mean_block, start, (blocks, id_blocks))
    centre = node_sums[:NODES] / node_counts[:NODES, None]
    centre_pad = jnp.concatenate([centre, jnp.zeros((SPAN_MOST, width), jnp.float32)], 0)
    frames_pad = jnp.broadcast_to(init_axes.astype(jnp.float32), (padded, width, AXES))
    for repeat in range(ITERS):

        def sweep_block(carry, item):
            block, node_ids = item
            first_node, member = window_member(node_ids)
            frames = lax.dynamic_slice_in_dim(frames_pad, first_node, SPAN_MOST, 0)
            centre_win = lax.dynamic_slice_in_dim(centre_pad, first_node, SPAN_MOST, 0)
            return (add_window(carry, first_node, local_moment(block, member, frames, centre_win)), None)
        moments, _ = lax.scan(sweep_block, jnp.zeros((padded, width, AXES), jnp.float32), (blocks, id_blocks))
        frames = jax.vmap(orthonormal)(moments[:NODES])
        frames_pad = jnp.concatenate([frames, jnp.zeros((SPAN_MOST, width, AXES), jnp.float32)], 0)

    def final_block(carry, item):
        block, node_ids = item
        first_node, member = window_member(node_ids)
        frames = lax.dynamic_slice_in_dim(frames_pad, first_node, SPAN_MOST, 0)
        centre_win = lax.dynamic_slice_in_dim(centre_pad, first_node, SPAN_MOST, 0)
        terms = lifted_terms(block, frames, centre_win)
        return (carry, lax.optimization_barrier(jnp.sum(terms * member[:, :, None], 1)))
    _, coords = lax.scan(final_block, jnp.float32(0.0), (blocks, id_blocks))
    return coords.reshape(TOTAL, AXES).T
```

```python
import functools

import jax
import jax.numpy as jnp
from jax import lax
from jax.experimental import pallas as pl
from jax.experimental.pallas import tpu as pltpu
from jax.sharding import PartitionSpec as P

AXES = 8
SLOTS = 8
WIDTH = 768
ROWS = 8192
COLS_N = 16
ROWS_N = 8
LANES = 128
TILES = WIDTH // LANES
LOAD = 1024
CHUNK = 2048
EXCHANGES = 3
f32 = jnp.float32
bf16 = jnp.bfloat16
NT = (((1,), (1,)), ((), ()))
NN = (((1,), (0,)), ((), ()))
MESH = pl.DeviceIdType.MESH


def split3(value):
    high = value.astype(bf16)
    rest = value - high.astype(f32)
    mid = rest.astype(bf16)
    low = (rest - mid.astype(f32)).astype(bf16)
    return jnp.concatenate([high, mid, low], 1)


def select_sum(weights, value):
    parts = lax.dot_general(weights, split3(value), NN, preferred_element_type=f32)
    return parts[:, :LANES] + parts[:, LANES : 2 * LANES] + parts[:, 2 * LANES :]


def kernel(
    points_ref,
    node_ref,
    init_ref,
    out_ref,
    x_ref,
    acc_ref,
    whole_ref,
    frame_ref,
    offset_ref,
    centre_ref,
    colsum_ref,
    mark_a,
    mark_b,
    mark_b_send,
    w_group,
    w_block,
    send_a,
    recv_a,
    send_b,
    recv_b,
    send_c,
    recv_c,
    load_sem,
    mark_sem,
    sem_a,
    sem_b,
    sem_c,
):
    row = lax.axis_index("row")
    col = lax.axis_index("col")

    def load(c):
        piece = pl.ds(c * LOAD, LOAD)
        return pltpu.make_async_copy(points_ref.at[piece, :], x_ref.at[piece, :], load_sem.at[c])

    for c in range(ROWS // LOAD):
        load(c).start()

    barrier = pltpu.get_barrier_semaphore()

    @pl.loop(1, COLS_N)
    def _(o):
        pl.semaphore_signal(
            barrier, inc=1, device_id=(row, lax.rem(col + o, COLS_N)), device_id_type=MESH
        )

    @pl.loop(1, ROWS_N)
    def _(o):
        pl.semaphore_signal(
            barrier, inc=1, device_id=(lax.rem(row + o, ROWS_N), col), device_id_type=MESH
        )

    def to_cols(source, target, sems):
        @pl.loop(1, COLS_N)
        def _(o):
            pltpu.make_async_remote_copy(
                src_ref=source(o),
                dst_ref=target(o),
                send_sem=sems.at[0],
                recv_sem=sems.at[1],
                device_id=(row, lax.rem(col + o, COLS_N)),
                device_id_type=MESH,
            ).start()

    def to_rows(source, target, sems):
        @pl.loop(1, ROWS_N)
        def _(o):
            pltpu.make_async_remote_copy(
                src_ref=source,
                dst_ref=target(o),
                send_sem=sems.at[0],
                recv_sem=sems.at[1],
                device_id=(lax.rem(row + o, ROWS_N), col),
                device_id_type=MESH,
            ).start()

    def settle(buffer, count, sem):
        some = buffer.at[pl.ds(1, count)]
        pltpu.make_async_copy(some, some, sem).wait()

    sub = lax.broadcasted_iota(jnp.int32, (8, LANES), 0)
    head_half = sub < 4
    first = jnp.broadcast_to(node_ref[0:1, 0:1], (8, LANES))
    last = jnp.broadcast_to(node_ref[0:1, ROWS - 1 : ROWS], (8, LANES))
    span = last - first
    mark_a[0] = jnp.where(head_half, first, last).astype(f32)

    base = init_ref[...].T
    base_bf = base.astype(bf16)
    base_pad = jnp.concatenate([base_bf, jnp.zeros_like(base_bf)], 0)
    acc_ref[...] = jnp.zeros_like(acc_ref)
    colsum_ref[...] = jnp.zeros_like(colsum_ref)

    def rel_of(start, size):
        ids = node_ref[:, pl.ds(start, size)]
        return jnp.broadcast_to(ids, (8, size)) - jnp.broadcast_to(first[:, 0:1], (8, size))

    def lane_sum(value):
        total = value[:, :LANES]
        for t in range(1, value.shape[1] // LANES):
            total = total + value[:, t * LANES : (t + 1) * LANES]
        return total

    def first_pass(c):
        load(c).wait()
        start = pl.multiple_of(c * LOAD, LOAD)
        x = x_ref[pl.ds(start, LOAD), :]
        s = lax.dot_general(base_pad, x, NT, preferred_element_type=f32)[:8]
        high = s.astype(bf16).astype(f32)
        low = s - high
        rel = rel_of(start, LOAD)
        sub_wide = lax.broadcasted_iota(jnp.int32, (8, LOAD), 0)
        member = jnp.where(rel == sub_wide, 1.0, 0.0)
        pieces = [jnp.where(rel == k, high, 0.0) for k in range(SLOTS)]
        pieces += [jnp.where(rel == k, low, 0.0) for k in range(SLOTS)]
        pieces += [member, jnp.zeros_like(member)]
        lifted = jnp.concatenate(pieces, 0).astype(bf16)
        acc_ref[...] += lax.dot_general(lifted, x, NN, preferred_element_type=f32)
        colsum_ref[0:8, :] += lane_sum(member)

    def first_range(lower, upper):
        @pl.loop(lower, upper)
        def _(c):
            first_pass(c)

    first_range(0, 2)
    pl.semaphore_wait(barrier, COLS_N - 1 + ROWS_N - 1)
    to_cols(lambda o: mark_a.at[0], lambda o: mark_a.at[o], mark_sem.at[0])
    first_range(2, 5)

    settle(mark_a, COLS_N - 1, mark_sem.at[0, 1])

    def voided(marks, count):
        other = pltpu.roll(marks, 4, 1)
        subs = lax.broadcasted_iota(jnp.int32, (count, 8, LANES), 1)
        return jnp.where((subs >= 4) & (marks == other), -1.0, marks)

    marks = mark_a[...]
    target = marks.reshape(LANES, LANES)
    sources = voided(marks, COLS_N).reshape(LANES, LANES).T
    like = (
        lax.rem(lax.broadcasted_iota(jnp.int32, (LANES, LANES), 0), 4)
        == lax.rem(lax.broadcasted_iota(jnp.int32, (LANES, LANES), 1), 4)
    )
    w_group[0:LANES, :] = jnp.where(like & (target == sources), 1.0, 0.0).astype(bf16)
    block_first = jnp.min(jnp.min(marks, 0), 0, keepdims=True)
    block_last = jnp.max(jnp.max(marks, 0), 0, keepdims=True)
    block_mark = jnp.where(head_half, block_first, block_last)
    block_rows = jnp.where(like[:8] & (block_mark == sources[:8]), 1.0, 0.0)
    w_group[LANES:, :] = jnp.concatenate([block_rows, jnp.zeros_like(block_rows)], 0).astype(bf16)
    mark_b_send[...] = block_mark
    mark_b[0] = jnp.full((8, LANES), -1.0, f32)
    to_rows(mark_b_send, lambda o: mark_b.at[o], mark_sem.at[1])
    first_range(5, 8)
    settle(mark_b, ROWS_N - 1, mark_sem.at[1, 1])
    marks_b = voided(mark_b[...], ROWS_N).reshape(8 * ROWS_N, LANES)
    marks_b = jnp.concatenate([marks_b, jnp.full((LANES - 8 * ROWS_N, LANES), -1.0, f32)], 0)
    block_sources = marks_b.T
    w_block[...] = jnp.where(like & (mark_a[...].reshape(LANES, LANES) == block_sources), 1.0, 0.0).astype(bf16)
    for e in range(EXCHANGES):
        recv_b[e, 0] = jnp.zeros((8, LANES), f32)

    def tile(t):
        return slice(t * LANES, (t + 1) * LANES)

    def spread_out(e, extra):
        head = acc_ref[0:8, :]
        tail = jnp.zeros_like(head)
        wide_span = jnp.broadcast_to(span[:, 0:1], (8, WIDTH))
        for k in range(1, SLOTS):
            tail = tail + jnp.where(wide_span == k, acc_ref[8 * k : 8 * k + 8, :], 0.0)
        for t in range(TILES):
            h, l = head[:, tile(t)], tail[:, tile(t)]
            send_a[e, 2 * t] = jnp.where(head_half, h, pltpu.roll(l, 4, 0))
            send_a[e, 2 * t + 1] = jnp.where(head_half, pltpu.roll(h, 4, 0), l)
        zero = jnp.zeros((8, LANES), f32)
        for m in range(2 * TILES, COLS_N):
            send_a[e, m] = zero
        if extra is not None:
            sums, counts = extra
            sub_wide = lax.broadcasted_iota(jnp.int32, (8, WIDTH), 0)
            sum_head = sums[0:1, :]
            sum_tail = jnp.sum(
                jnp.where((sub_wide == wide_span) & (sub_wide > 0), sums, 0.0), 0, keepdims=True
            )
            for t in range(TILES):
                m, r = 2 * TILES + t // 4, t % 4
                send_a[e, m, r : r + 1, :] = sum_head[:, tile(t)]
                send_a[e, m, r + 4 : r + 5, :] = sum_tail[:, tile(t)]
            count_head = counts[0:1, :]
            count_tail = jnp.sum(jnp.where((sub == span) & (sub > 0), counts, 0.0), 0, keepdims=True)
            send_a[e, 2 * TILES + 2] = jnp.where(
                head_half,
                jnp.broadcast_to(count_head, (8, LANES)),
                jnp.broadcast_to(count_tail, (8, LANES)),
            )

    def exchange(e):
        recv_a[e, 0] = send_a[e, col]
        to_cols(
            lambda o: send_a.at[e, lax.rem(col + o, COLS_N)],
            lambda o: recv_a.at[e, o],
            sem_a.at[e],
        )
        settle(recv_a.at[e], COLS_N - 1, sem_a.at[e, 1])
        group = select_sum(w_group[...], recv_a[e].reshape(LANES, LANES))
        send_b[e] = group[LANES : LANES + 8]
        to_rows(send_b.at[e], lambda o: recv_b.at[e, o], sem_b.at[e])
        settle(recv_b.at[e], ROWS_N - 1, sem_b.at[e, 1])
        blocks = recv_b[e].reshape(8 * ROWS_N, LANES)
        blocks = jnp.concatenate([blocks, jnp.zeros((LANES - 8 * ROWS_N, LANES), f32)], 0)
        whole = group[:LANES] + select_sum(w_block[...], blocks)
        send_c[e] = whole.reshape(COLS_N, 8, LANES)
        recv_c[e, col] = send_c[e, 0]
        @pl.loop(1, COLS_N)
        def _(o):
            pltpu.make_async_remote_copy(
                src_ref=send_c.at[e, o],
                dst_ref=recv_c.at[e, col],
                send_sem=sem_c.at[e, 0],
                recv_sem=sem_c.at[e, 1],
                device_id=(row, lax.rem(col - o + COLS_N, COLS_N)),
                device_id_type=MESH,
            ).start()
        settle(recv_c.at[e], COLS_N - 1, sem_c.at[e, 1])

    def gather_in(e):
        heads, tails = [], []
        for t in range(TILES):
            a, b = recv_c[e, 2 * t], recv_c[e, 2 * t + 1]
            heads.append(jnp.where(head_half, a, pltpu.roll(b, 4, 0)))
            tails.append(jnp.where(head_half, pltpu.roll(a, 4, 0), b))
        for t in range(TILES):
            whole_ref[t, 0:8, :] = heads[t]
            for k in range(1, SLOTS):
                whole_ref[t, 8 * k : 8 * k + 8, :] = jnp.where(
                    span == k, tails[t], acc_ref[8 * k : 8 * k + 8, tile(t)]
                )

    def take(k):
        return jnp.concatenate(
            [whole_ref[t, pl.ds(k, SLOTS, stride=AXES), :] for t in range(TILES)], 1
        )

    live = sub <= span

    def orthonormal(vectors):
        centre = centre_ref[...]
        for k in range(AXES):
            vector = vectors[k]
            square = jnp.sum(vector * vector, 1, keepdims=True)
            square = jnp.where(live[:, 0:1], square, 1.0)
            inverse = 1.0 / square
            for j in range(k + 1, AXES):
                along = jnp.sum(vector * vectors[j], 1, keepdims=True) * inverse
                vectors[j] = vectors[j] - along * vector
            unit = vector * (1.0 / jnp.sqrt(square))
            for t in range(TILES):
                frame_ref[t, pl.ds(k, SLOTS, stride=AXES), :] = unit[:, tile(t)]
            offset = jnp.sum(unit * centre, 1, keepdims=True)
            offset_ref[pl.ds(k, SLOTS, stride=AXES), :] = jnp.broadcast_to(offset, (8, LANES))

    acc_ref[0:64, :] = acc_ref[0:64, :] + acc_ref[64:128, :]
    counts = jnp.broadcast_to(jnp.sum(colsum_ref[0:8, :], 1, keepdims=True), (8, LANES))
    sums = acc_ref[128:136, :]
    spread_out(0, (sums, counts))
    exchange(0)
    gather_in(0)
    heads = [recv_c[0, 2 * TILES + t // 4, t % 4 : t % 4 + 1, :] for t in range(TILES)]
    tails = [recv_c[0, 2 * TILES + t // 4, t % 4 + 4 : t % 4 + 5, :] for t in range(TILES)]
    sub_wide = lax.broadcasted_iota(jnp.int32, (8, WIDTH), 0)
    wide_span = jnp.broadcast_to(span[:, 0:1], (8, WIDTH))
    sums = jnp.where(sub_wide == wide_span, jnp.concatenate(tails, 1), sums)
    sums = jnp.where(sub_wide == 0, jnp.concatenate(heads, 1), sums)
    counts = jnp.where(sub == span, recv_c[0, 2 * TILES + 2, 4:5, :], counts)
    counts = jnp.where(sub == 0, recv_c[0, 2 * TILES + 2, 0:1, :], counts)
    counts = jnp.where(live, counts, 1.0)
    centre = sums / counts[:, 0:1]
    centre_ref[...] = centre
    base_used = base_bf.astype(f32)
    vectors = []
    for k in range(AXES):
        total = jnp.sum(sums * base_used[k : k + 1, :], 1, keepdims=True)
        vectors.append(take(k) - total * centre)
    orthonormal(vectors)

    def frame_used():
        return jnp.concatenate([frame_ref[t] for t in range(TILES)], 1).astype(bf16)

    for e in range(1, EXCHANGES):
        frame = frame_used()
        acc_ref[0:64, :] = jnp.zeros((64, WIDTH), f32)
        colsum_ref[...] = jnp.zeros_like(colsum_ref)

        @pl.loop(0, ROWS // CHUNK)
        def _(c):
            start = pl.multiple_of(c * CHUNK, CHUNK)
            x = x_ref[pl.ds(start, CHUNK), :]
            s = lax.dot_general(frame, x, NT, preferred_element_type=f32)
            rel = rel_of(start, CHUNK)
            pieces = [
                jnp.where(
                    rel == k,
                    s[8 * k : 8 * k + 8]
                    - jnp.broadcast_to(offset_ref[8 * k : 8 * k + 8, 0:1], (8, CHUNK)),
                    0.0,
                )
                for k in range(SLOTS)
            ]
            lifted = jnp.concatenate(pieces, 0).astype(bf16)
            acc_ref[0:64, :] += lax.dot_general(lifted, x, NN, preferred_element_type=f32)
            colsum_ref[...] += lane_sum(lifted.astype(f32))

        column_sums = jnp.sum(colsum_ref[...], 1, keepdims=True)
        for k in range(SLOTS):
            acc_ref[8 * k : 8 * k + 8, :] -= column_sums[8 * k : 8 * k + 8] * centre_ref[k : k + 1, :]
        spread_out(e, None)
        exchange(e)
        gather_in(e)
        orthonormal([take(k) for k in range(AXES)])

    frame = frame_used()

    @pl.loop(0, ROWS // CHUNK)
    def _(c):
        start = pl.multiple_of(c * CHUNK, CHUNK)
        x = x_ref[pl.ds(start, CHUNK), :]
        s = lax.dot_general(frame, x, NT, preferred_element_type=f32)
        rel = rel_of(start, CHUNK)
        found = jnp.zeros((8, CHUNK), f32)
        for k in range(SLOTS):
            centred = s[8 * k : 8 * k + 8] - jnp.broadcast_to(
                offset_ref[8 * k : 8 * k + 8, 0:1], (8, CHUNK)
            )
            found = jnp.where(rel == k, centred, found)
        out_ref[:, pl.ds(start, CHUNK)] = found

    settle(mark_a, COLS_N - 1, mark_sem.at[0, 0])
    settle(mark_b, ROWS_N - 1, mark_sem.at[1, 0])
    for e in range(EXCHANGES):
        settle(recv_a.at[e], COLS_N - 1, sem_a.at[e, 0])
        settle(recv_b.at[e], ROWS_N - 1, sem_b.at[e, 0])
        settle(recv_c.at[e], COLS_N - 1, sem_c.at[e, 0])


def shards(points, node_of_row, init_axes):
    vmem = pl.BlockSpec(memory_space=pltpu.VMEM)
    DMA = pltpu.SemaphoreType.DMA
    return pl.pallas_call(
        kernel,
        out_shape=jax.ShapeDtypeStruct((AXES, ROWS), f32),
        in_specs=[pl.BlockSpec(memory_space=pl.ANY), vmem, vmem],
        out_specs=vmem,
        scratch_shapes=[
            pltpu.VMEM((ROWS, WIDTH), bf16),
            pltpu.VMEM((144, WIDTH), f32),
            pltpu.VMEM((TILES, 64, LANES), f32),
            pltpu.VMEM((TILES, 64, LANES), f32),
            pltpu.VMEM((64, LANES), f32),
            pltpu.VMEM((SLOTS, WIDTH), f32),
            pltpu.VMEM((64, LANES), f32),
            pltpu.VMEM((COLS_N, 8, LANES), f32),
            pltpu.VMEM((ROWS_N, 8, LANES), f32),
            pltpu.VMEM((8, LANES), f32),
            pltpu.VMEM((144, LANES), bf16),
            pltpu.VMEM((LANES, LANES), bf16),
            pltpu.VMEM((EXCHANGES, COLS_N, 8, LANES), f32),
            pltpu.VMEM((EXCHANGES, COLS_N, 8, LANES), f32),
            pltpu.VMEM((EXCHANGES, 8, LANES), f32),
            pltpu.VMEM((EXCHANGES, ROWS_N, 8, LANES), f32),
            pltpu.VMEM((EXCHANGES, COLS_N, 8, LANES), f32),
            pltpu.VMEM((EXCHANGES, COLS_N, 8, LANES), f32),
            DMA((ROWS // LOAD,)),
            DMA((2, 2)),
            DMA((EXCHANGES, 2)),
            DMA((EXCHANGES, 2)),
            DMA((EXCHANGES, 2)),
        ],
        compiler_params=pltpu.CompilerParams(
            collective_id=0, has_side_effects=True, vmem_limit_bytes=56 * 2**20
        ),
        name="principal_axes",
    )(points, node_of_row.reshape(1, ROWS), init_axes)


def solution(mesh):
    return jax.shard_map(
        shards,
        mesh=mesh,
        in_specs=(P(("row", "col"), None), P(("row", "col")), P()),
        out_specs=P(None, ("row", "col")),
        check_vma=False,
    )
```

```python
import functools

import jax
import jax.numpy as jnp
from jax import lax
from jax.experimental import pallas as pl
from jax.experimental.pallas import tpu as pltpu
from jax.sharding import PartitionSpec as P

AXES = 8
SLOTS = 8
WIDTH = 768
ROWS = 8192
COLS_N = 16
ROWS_N = 8
LANES = 128
TILES = WIDTH // LANES
LOAD = 1024
CHUNK = 4096
EXCHANGES = 3
f32 = jnp.float32
bf16 = jnp.bfloat16
NT = (((1,), (1,)), ((), ()))
NN = (((1,), (0,)), ((), ()))
MESH = pl.DeviceIdType.MESH


def split3(value):
    high = value.astype(bf16)
    rest = value - high.astype(f32)
    mid = rest.astype(bf16)
    low = (rest - mid.astype(f32)).astype(bf16)
    return jnp.concatenate([high, mid, low], 1)


def select_sum(weights, parts):
    parts = lax.dot_general(weights, parts, NN, preferred_element_type=f32)
    return parts[:, :LANES] + parts[:, LANES : 2 * LANES] + parts[:, 2 * LANES :]


def kernel(
    points_ref,
    node_ref,
    init_ref,
    out_ref,
    x_ref,
    xt_ref,
    acc_ref,
    whole_ref,
    frame_ref,
    offset_ref,
    centre_ref,
    colsum_ref,
    mark_a,
    mark_b,
    mark_b_send,
    w_group,
    w_block,
    send_a,
    recv_a,
    send_b,
    recv_b,
    send_c,
    recv_c,
    load_sem,
    mark_sem,
    sem_a,
    sem_b,
    sem_c,
):
    row = lax.axis_index("row")
    col = lax.axis_index("col")

    def load(c):
        piece = pl.ds(c * LOAD, LOAD)
        return pltpu.make_async_copy(points_ref.at[piece, :], x_ref.at[piece, :], load_sem.at[c])

    for c in range(ROWS // LOAD):
        load(c).start()

    barrier = pltpu.get_barrier_semaphore()

    @pl.loop(1, COLS_N)
    def _(o):
        pl.semaphore_signal(
            barrier, inc=1, device_id=(row, lax.rem(col + o, COLS_N)), device_id_type=MESH
        )

    @pl.loop(1, ROWS_N)
    def _(o):
        pl.semaphore_signal(
            barrier, inc=1, device_id=(lax.rem(row + o, ROWS_N), col), device_id_type=MESH
        )

    def to_cols(source, target, sems):
        @pl.loop(1, COLS_N)
        def _(o):
            pltpu.make_async_remote_copy(
                src_ref=source(o),
                dst_ref=target(o),
                send_sem=sems.at[0],
                recv_sem=sems.at[1],
                device_id=(row, lax.rem(col + o, COLS_N)),
                device_id_type=MESH,
            ).start()

    def to_rows(source, target, sems):
        @pl.loop(1, ROWS_N)
        def _(o):
            pltpu.make_async_remote_copy(
                src_ref=source,
                dst_ref=target(o),
                send_sem=sems.at[0],
                recv_sem=sems.at[1],
                device_id=(lax.rem(row + o, ROWS_N), col),
                device_id_type=MESH,
            ).start()

    def settle(buffer, count, sem):
        some = buffer.at[pl.ds(1, count)]
        pltpu.make_async_copy(some, some, sem).wait()

    sub = lax.broadcasted_iota(jnp.int32, (8, LANES), 0)
    head_half = sub < 4
    first = jnp.broadcast_to(node_ref[0:1, 0:1], (8, LANES))
    last = jnp.broadcast_to(node_ref[0:1, ROWS - 1 : ROWS], (8, LANES))
    span = last - first
    mark_a[0] = jnp.where(head_half, first, last).astype(f32)

    base = init_ref[...]
    base_bf = base.astype(bf16)
    base_pad = jnp.concatenate([base_bf, jnp.zeros_like(base_bf)], 0)
    acc_ref[...] = jnp.zeros_like(acc_ref)
    colsum_ref[...] = jnp.zeros_like(colsum_ref)

    def rel_of(start, size):
        ids = node_ref[:, pl.ds(start, size)]
        return jnp.broadcast_to(ids, (8, size)) - jnp.broadcast_to(first[:, 0:1], (8, size))

    def lane_sum(value):
        total = value[:, :LANES]
        for t in range(1, value.shape[1] // LANES):
            total = total + value[:, t * LANES : (t + 1) * LANES]
        return total

    def first_pass(c):
        load(c).wait()
        start = pl.multiple_of(c * LOAD, LOAD)
        x = x_ref[pl.ds(start, LOAD), :]
        xt = x.T
        xt_ref[:, pl.ds(start, LOAD)] = xt
        s = lax.dot_general(base_pad, xt, NN, preferred_element_type=f32)[:8]
        high = s.astype(bf16).astype(f32)
        low = s - high
        rel = rel_of(start, LOAD)
        sub_wide = lax.broadcasted_iota(jnp.int32, (8, LOAD), 0)
        member = jnp.where(rel == sub_wide, 1.0, 0.0)
        pieces = [jnp.where(rel == k, high, 0.0) for k in range(SLOTS)]
        pieces += [jnp.where(rel == k, low, 0.0) for k in range(SLOTS)]
        pieces += [member, jnp.zeros_like(member)]
        lifted = jnp.concatenate(pieces, 0).astype(bf16)
        acc_ref[...] += lax.dot_general(lifted, x, NN, preferred_element_type=f32)
        colsum_ref[0:8, :] += lane_sum(member)

    def first_range(lower, upper):
        @pl.loop(lower, upper)
        def _(c):
            first_pass(c)

    first_range(0, 2)
    pl.semaphore_wait(barrier, COLS_N - 1 + ROWS_N - 1)
    to_cols(lambda o: mark_a.at[0], lambda o: mark_a.at[o], mark_sem.at[0])
    first_range(2, ROWS // LOAD)
    like = (
        lax.rem(lax.broadcasted_iota(jnp.int32, (LANES, LANES), 0), 4)
        == lax.rem(lax.broadcasted_iota(jnp.int32, (LANES, LANES), 1), 4)
    )

    def voided(marks, count):
        other = pltpu.roll(marks, 4, 1)
        subs = lax.broadcasted_iota(jnp.int32, (count, 8, LANES), 1)
        return jnp.where((subs >= 4) & (marks == other), -1.0, marks)

    def group_weights():
        settle(mark_a, COLS_N - 1, mark_sem.at[0, 1])
        marks = mark_a[...]
        target = marks.reshape(LANES, LANES)
        sources = voided(marks, COLS_N).reshape(LANES, LANES).T
        w_group[16:, :] = jnp.where(like & (target == sources), 1.0, 0.0).astype(bf16)
        block_first = jnp.min(jnp.min(marks, 0), 0, keepdims=True)
        block_last = jnp.max(jnp.max(marks, 0), 0, keepdims=True)
        block_mark = jnp.where(head_half, block_first, block_last)
        block_rows = jnp.where(like[:8] & (block_mark == sources[:8]), 1.0, 0.0)
        w_group[0:16, :] = jnp.concatenate([block_rows, jnp.zeros_like(block_rows)], 0).astype(bf16)
        mark_b_send[...] = block_mark
        mark_b[0] = jnp.full((8, LANES), -1.0, f32)

    def block_weights():
        settle(mark_b, ROWS_N - 1, mark_sem.at[1, 1])
        marks_b = voided(mark_b[...], ROWS_N).reshape(8 * ROWS_N, LANES)
        marks_b = jnp.concatenate(
            [marks_b, jnp.full((LANES - 8 * ROWS_N, LANES), -1.0, f32)], 0
        )
        target = mark_a[...].reshape(LANES, LANES)
        w_block[...] = jnp.where(like & (target == marks_b.T), 1.0, 0.0).astype(bf16)

    for e in range(EXCHANGES):
        recv_b[e, 0] = jnp.zeros((8, LANES), f32)

    def tile(t):
        return slice(t * LANES, (t + 1) * LANES)

    def spread_out(e, extra):
        head = acc_ref[0:8, :]
        tail = jnp.zeros_like(head)
        wide_span = jnp.broadcast_to(span[:, 0:1], (8, WIDTH))
        for k in range(1, SLOTS):
            tail = tail + jnp.where(wide_span == k, acc_ref[8 * k : 8 * k + 8, :], 0.0)
        for t in range(TILES):
            h, l = head[:, tile(t)], tail[:, tile(t)]
            send_a[e, 2 * t] = jnp.where(head_half, h, pltpu.roll(l, 4, 0))
            send_a[e, 2 * t + 1] = jnp.where(head_half, pltpu.roll(h, 4, 0), l)
        zero = jnp.zeros((8, LANES), f32)
        for m in range(2 * TILES, COLS_N):
            send_a[e, m] = zero
        if extra is not None:
            sums, counts = extra
            sub_wide = lax.broadcasted_iota(jnp.int32, (8, WIDTH), 0)
            sum_head = sums[0:1, :]
            sum_tail = jnp.sum(
                jnp.where((sub_wide == wide_span) & (sub_wide > 0), sums, 0.0), 0, keepdims=True
            )
            for t in range(TILES):
                m, r = 2 * TILES + t // 4, t % 4
                send_a[e, m, r : r + 1, :] = sum_head[:, tile(t)]
                send_a[e, m, r + 4 : r + 5, :] = sum_tail[:, tile(t)]
            count_head = counts[0:1, :]
            count_tail = jnp.sum(jnp.where((sub == span) & (sub > 0), counts, 0.0), 0, keepdims=True)
            send_a[e, 2 * TILES + 2] = jnp.where(
                head_half,
                jnp.broadcast_to(count_head, (8, LANES)),
                jnp.broadcast_to(count_tail, (8, LANES)),
            )

    def exchange(e):
        recv_a[e, 0] = send_a[e, col]
        to_cols(
            lambda o: send_a.at[e, lax.rem(col + o, COLS_N)],
            lambda o: recv_a.at[e, o],
            sem_a.at[e],
        )
        if e == 0:
            group_weights()
        settle(recv_a.at[e], COLS_N - 1, sem_a.at[e, 1])
        parts = split3(recv_a[e].reshape(LANES, LANES))
        send_b[e] = select_sum(w_group[0:16, :], parts)[:8]
        to_rows(send_b.at[e], lambda o: recv_b.at[e, o], sem_b.at[e])
        if e == 0:
            to_rows(mark_b_send, lambda o: mark_b.at[o], mark_sem.at[1])
        group = select_sum(w_group[16:, :], parts)
        settle(recv_b.at[e], ROWS_N - 1, sem_b.at[e, 1])
        if e == 0:
            block_weights()
        blocks = recv_b[e].reshape(8 * ROWS_N, LANES)
        blocks = jnp.concatenate([blocks, jnp.zeros((LANES - 8 * ROWS_N, LANES), f32)], 0)
        whole = group + select_sum(w_block[...], split3(blocks))
        send_c[e] = whole.reshape(COLS_N, 8, LANES)
        recv_c[e, col] = send_c[e, 0]
        @pl.loop(1, COLS_N)
        def _(o):
            pltpu.make_async_remote_copy(
                src_ref=send_c.at[e, o],
                dst_ref=recv_c.at[e, col],
                send_sem=sem_c.at[e, 0],
                recv_sem=sem_c.at[e, 1],
                device_id=(row, lax.rem(col - o + COLS_N, COLS_N)),
                device_id_type=MESH,
            ).start()
        settle(recv_c.at[e], COLS_N - 1, sem_c.at[e, 1])

    def gather_in(e):
        heads, tails = [], []
        for t in range(TILES):
            a, b = recv_c[e, 2 * t], recv_c[e, 2 * t + 1]
            heads.append(jnp.where(head_half, a, pltpu.roll(b, 4, 0)))
            tails.append(jnp.where(head_half, pltpu.roll(a, 4, 0), b))
        for t in range(TILES):
            whole_ref[t, 0:8, :] = heads[t]
            for k in range(1, SLOTS):
                whole_ref[t, 8 * k : 8 * k + 8, :] = jnp.where(
                    span == k, tails[t], acc_ref[8 * k : 8 * k + 8, tile(t)]
                )

    def take(k):
        return jnp.concatenate(
            [whole_ref[t, pl.ds(k, SLOTS, stride=AXES), :] for t in range(TILES)], 1
        )

    live = sub <= span

    def orthonormal(vectors):
        centre = centre_ref[...]
        for k in range(AXES):
            vector = vectors[k]
            square = jnp.sum(vector * vector, 1, keepdims=True)
            square = jnp.where(live[:, 0:1], square, 1.0)
            inverse = 1.0 / square
            for j in range(k + 1, AXES):
                along = jnp.sum(vector * vectors[j], 1, keepdims=True) * inverse
                vectors[j] = vectors[j] - along * vector
            unit = vector * (1.0 / jnp.sqrt(square))
            for t in range(TILES):
                frame_ref[t, pl.ds(k, SLOTS, stride=AXES), :] = unit[:, tile(t)]
            offset = jnp.sum(unit * centre, 1, keepdims=True)
            offset_ref[pl.ds(k, SLOTS, stride=AXES), :] = jnp.broadcast_to(offset, (8, LANES))

    acc_ref[0:64, :] = acc_ref[0:64, :] + acc_ref[64:128, :]
    counts = jnp.broadcast_to(jnp.sum(colsum_ref[0:8, :], 1, keepdims=True), (8, LANES))
    sums = acc_ref[128:136, :]
    spread_out(0, (sums, counts))
    exchange(0)
    gather_in(0)
    heads = [recv_c[0, 2 * TILES + t // 4, t % 4 : t % 4 + 1, :] for t in range(TILES)]
    tails = [recv_c[0, 2 * TILES + t // 4, t % 4 + 4 : t % 4 + 5, :] for t in range(TILES)]
    sub_wide = lax.broadcasted_iota(jnp.int32, (8, WIDTH), 0)
    wide_span = jnp.broadcast_to(span[:, 0:1], (8, WIDTH))
    sums = jnp.where(sub_wide == wide_span, jnp.concatenate(tails, 1), sums)
    sums = jnp.where(sub_wide == 0, jnp.concatenate(heads, 1), sums)
    counts = jnp.where(sub == span, recv_c[0, 2 * TILES + 2, 4:5, :], counts)
    counts = jnp.where(sub == 0, recv_c[0, 2 * TILES + 2, 0:1, :], counts)
    counts = jnp.where(live, counts, 1.0)
    centre = sums / counts[:, 0:1]
    centre_ref[...] = centre
    base_used = base_bf.astype(f32)
    vectors = []
    for k in range(AXES):
        total = jnp.sum(sums * base_used[k : k + 1, :], 1, keepdims=True)
        vectors.append(take(k) - total * centre)
    orthonormal(vectors)

    def frame_used():
        return jnp.concatenate([frame_ref[t] for t in range(TILES)], 1).astype(bf16)

    for e in range(1, EXCHANGES):
        frame = frame_used()
        acc_ref[0:64, :] = jnp.zeros((64, WIDTH), f32)
        colsum_ref[...] = jnp.zeros_like(colsum_ref)

        @pl.loop(0, ROWS // CHUNK)
        def _(c):
            start = pl.multiple_of(c * CHUNK, CHUNK)
            x = x_ref[pl.ds(start, CHUNK), :]
            s = lax.dot_general(
                frame, xt_ref[:, pl.ds(start, CHUNK)], NN, preferred_element_type=f32
            )
            rel = rel_of(start, CHUNK)
            pieces = [
                jnp.where(
                    rel == k,
                    s[8 * k : 8 * k + 8]
                    - jnp.broadcast_to(offset_ref[8 * k : 8 * k + 8, 0:1], (8, CHUNK)),
                    0.0,
                )
                for k in range(SLOTS)
            ]
            lifted = jnp.concatenate(pieces, 0).astype(bf16)
            acc_ref[0:64, :] += lax.dot_general(lifted, x, NN, preferred_element_type=f32)
            colsum_ref[...] += lane_sum(lifted.astype(f32))

        column_sums = jnp.sum(colsum_ref[...], 1, keepdims=True)
        for k in range(SLOTS):
            acc_ref[8 * k : 8 * k + 8, :] -= column_sums[8 * k : 8 * k + 8] * centre_ref[k : k + 1, :]
        spread_out(e, None)
        exchange(e)
        gather_in(e)
        orthonormal([take(k) for k in range(AXES)])

    frame = frame_used()

    @pl.loop(0, ROWS // CHUNK)
    def _(c):
        start = pl.multiple_of(c * CHUNK, CHUNK)
        s = lax.dot_general(
            frame, xt_ref[:, pl.ds(start, CHUNK)], NN, preferred_element_type=f32
        )
        rel = rel_of(start, CHUNK)
        found = jnp.zeros((8, CHUNK), f32)
        for k in range(SLOTS):
            centred = s[8 * k : 8 * k + 8] - jnp.broadcast_to(
                offset_ref[8 * k : 8 * k + 8, 0:1], (8, CHUNK)
            )
            found = jnp.where(rel == k, centred, found)
        out_ref[:, pl.ds(start, CHUNK)] = found

    settle(mark_a, COLS_N - 1, mark_sem.at[0, 0])
    settle(mark_b, ROWS_N - 1, mark_sem.at[1, 0])
    for e in range(EXCHANGES):
        settle(recv_a.at[e], COLS_N - 1, sem_a.at[e, 0])
        settle(recv_b.at[e], ROWS_N - 1, sem_b.at[e, 0])
        settle(recv_c.at[e], COLS_N - 1, sem_c.at[e, 0])


def shards(points, node_of_row, init_axes):
    vmem = pl.BlockSpec(memory_space=pltpu.VMEM)
    DMA = pltpu.SemaphoreType.DMA
    return pl.pallas_call(
        kernel,
        out_shape=jax.ShapeDtypeStruct((AXES, ROWS), f32),
        in_specs=[pl.BlockSpec(memory_space=pl.ANY), vmem, vmem],
        out_specs=vmem,
        scratch_shapes=[
            pltpu.VMEM((ROWS, WIDTH), bf16),
            pltpu.VMEM((WIDTH, ROWS), bf16),
            pltpu.VMEM((144, WIDTH), f32),
            pltpu.VMEM((TILES, 64, LANES), f32),
            pltpu.VMEM((TILES, 64, LANES), f32),
            pltpu.VMEM((64, LANES), f32),
            pltpu.VMEM((SLOTS, WIDTH), f32),
            pltpu.VMEM((64, LANES), f32),
            pltpu.VMEM((COLS_N, 8, LANES), f32),
            pltpu.VMEM((ROWS_N, 8, LANES), f32),
            pltpu.VMEM((8, LANES), f32),
            pltpu.VMEM((144, LANES), bf16),
            pltpu.VMEM((LANES, LANES), bf16),
            pltpu.VMEM((EXCHANGES, COLS_N, 8, LANES), f32),
            pltpu.VMEM((EXCHANGES, COLS_N, 8, LANES), f32),
            pltpu.VMEM((EXCHANGES, 8, LANES), f32),
            pltpu.VMEM((EXCHANGES, ROWS_N, 8, LANES), f32),
            pltpu.VMEM((EXCHANGES, COLS_N, 8, LANES), f32),
            pltpu.VMEM((EXCHANGES, COLS_N, 8, LANES), f32),
            DMA((ROWS // LOAD,)),
            DMA((2, 2)),
            DMA((EXCHANGES, 2)),
            DMA((EXCHANGES, 2)),
            DMA((EXCHANGES, 2)),
        ],
        compiler_params=pltpu.CompilerParams(
            collective_id=0, has_side_effects=True, vmem_limit_bytes=53 * 2**20
        ),
        name="principal_axes",
    )(points, node_of_row.reshape(1, ROWS), init_axes.T)


def solution(mesh):
    return jax.shard_map(
        shards,
        mesh=mesh,
        in_specs=(P(("row", "col"), None), P(("row", "col")), P()),
        out_specs=P(None, ("row", "col")),
        check_vma=False,
    )
```

```python
import functools

import jax
import jax.numpy as jnp
from jax import lax
from jax.experimental import pallas as pl
from jax.experimental.pallas import tpu as pltpu
from jax.sharding import PartitionSpec as P

AXES = 8
SLOTS = 8
WIDTH = 768
ROWS = 8192
COLS_N = 16
ROWS_N = 8
LANES = 128
TILES = WIDTH // LANES
LOAD = 1024
FIRST = 2048
CHUNK = 4096
EXCHANGES = 3
SIDE = 4


def hops(o):
    return min(o, SIDE - o)


FAR_COLS = sorted(range(1, COLS_N), key=lambda o: -hops(o // SIDE) - hops(o % SIDE))
FAR_ROWS = sorted(range(1, ROWS_N), key=lambda o: -hops(o // 2))
f32 = jnp.float32
bf16 = jnp.bfloat16
NT = (((1,), (1,)), ((), ()))
NN = (((1,), (0,)), ((), ()))
MESH = pl.DeviceIdType.MESH


def split3(value):
    high = value.astype(bf16)
    rest = value - high.astype(f32)
    mid = rest.astype(bf16)
    low = (rest - mid.astype(f32)).astype(bf16)
    return jnp.concatenate([high, mid, low], 1)


def select_sum(weights, parts):
    parts = lax.dot_general(weights, parts, NN, preferred_element_type=f32)
    return parts[:, :LANES] + parts[:, LANES : 2 * LANES] + parts[:, 2 * LANES :]


def kernel(
    points_ref,
    node_ref,
    init_ref,
    out_ref,
    x_ref,
    xt_ref,
    acc_ref,
    whole_ref,
    frame_ref,
    offset_ref,
    centre_ref,
    colsum_ref,
    mark_a,
    mark_b,
    mark_b_send,
    w_group,
    w_block,
    send_a,
    recv_a,
    send_b,
    recv_b,
    send_c,
    recv_c,
    load_sem,
    mark_sem,
    sem_a,
    sem_b,
    sem_c,
):
    row = lax.axis_index("row")
    col = lax.axis_index("col")

    def load(c):
        piece = pl.ds(c * LOAD, LOAD)
        return pltpu.make_async_copy(points_ref.at[piece, :], x_ref.at[piece, :], load_sem.at[c])

    for c in range(ROWS // LOAD):
        load(c).start()

    barrier = pltpu.get_barrier_semaphore()

    def col_at(o, sign=1):
        x = lax.rem(col // SIDE + sign * (o // SIDE) + SIDE, SIDE)
        z = lax.rem(lax.rem(col, SIDE) + sign * (o % SIDE) + SIDE, SIDE)
        return x * SIDE + z

    for o in FAR_COLS:
        pl.semaphore_signal(
            barrier, inc=1, device_id=(row, col_at(o)), device_id_type=MESH
        )

    for o in FAR_ROWS:
        pl.semaphore_signal(
            barrier, inc=1, device_id=(lax.rem(row + o, ROWS_N), col), device_id_type=MESH
        )

    def to_cols(source, target, sems):
        for o in FAR_COLS:
            pltpu.make_async_remote_copy(
                src_ref=source(o),
                dst_ref=target(o),
                send_sem=sems.at[0],
                recv_sem=sems.at[1],
                device_id=(row, col_at(o)),
                device_id_type=MESH,
            ).start()

    def to_rows(source, target, sems):
        for o in FAR_ROWS:
            pltpu.make_async_remote_copy(
                src_ref=source,
                dst_ref=target(o),
                send_sem=sems.at[0],
                recv_sem=sems.at[1],
                device_id=(lax.rem(row + o, ROWS_N), col),
                device_id_type=MESH,
            ).start()

    def settle(buffer, count, sem):
        some = buffer.at[pl.ds(1, count)]
        pltpu.make_async_copy(some, some, sem).wait()

    sub = lax.broadcasted_iota(jnp.int32, (8, LANES), 0)
    head_half = sub < 4
    first = jnp.broadcast_to(node_ref[0:1, 0:1], (8, LANES))
    last = jnp.broadcast_to(node_ref[0:1, ROWS - 1 : ROWS], (8, LANES))
    span = last - first
    mark_a[0] = jnp.where(head_half, first, last).astype(f32)

    base = init_ref[...]
    base_bf = base.astype(bf16)
    base_pad = jnp.concatenate([base_bf, jnp.zeros_like(base_bf)], 0)
    acc_ref[...] = jnp.zeros_like(acc_ref)
    colsum_ref[...] = jnp.zeros_like(colsum_ref)

    def rel_of(start, size):
        ids = node_ref[:, pl.ds(start, size)]
        return jnp.broadcast_to(ids, (8, size)) - jnp.broadcast_to(first[:, 0:1], (8, size))

    def lane_sum(value):
        total = value[:, :LANES]
        for t in range(1, value.shape[1] // LANES):
            total = total + value[:, t * LANES : (t + 1) * LANES]
        return total

    def first_pass(c, n):
        FIRST = n * LOAD
        for part in range(n):
            load(c + part).wait()
        start = pl.multiple_of(c * LOAD, LOAD)
        x = x_ref[pl.ds(start, FIRST), :]
        xt = x.T
        xt_ref[:, pl.ds(start, FIRST)] = xt
        s = lax.dot_general(base_pad, xt, NN, preferred_element_type=f32)[:8]
        high = s.astype(bf16).astype(f32)
        low = s - high
        rel = rel_of(start, FIRST)
        sub_wide = lax.broadcasted_iota(jnp.int32, (8, FIRST), 0)
        member = jnp.where(rel == sub_wide, 1.0, 0.0)
        pieces = [jnp.where(rel == k, high, 0.0) for k in range(SLOTS)]
        pieces += [jnp.where(rel == k, low, 0.0) for k in range(SLOTS)]
        pieces += [member, jnp.zeros_like(member)]
        lifted = jnp.concatenate(pieces, 0).astype(bf16)
        acc_ref[...] += lax.dot_general(lifted, x, NN, preferred_element_type=f32)
        colsum_ref[0:8, :] += lane_sum(member)

    def first_range(lower, upper):
        first_pass(0, 1)
        first_pass(1, 1)

        @pl.loop(1, 4)
        def _(c):
            first_pass(2 * c, 2)

    first_range(0, ROWS // FIRST)
    pl.semaphore_wait(barrier, COLS_N - 1 + ROWS_N - 1)
    to_cols(lambda o: mark_a.at[0], lambda o: mark_a.at[o], mark_sem.at[0])
    like = (
        lax.rem(lax.broadcasted_iota(jnp.int32, (LANES, LANES), 0), 4)
        == lax.rem(lax.broadcasted_iota(jnp.int32, (LANES, LANES), 1), 4)
    )

    def voided(marks, count):
        other = pltpu.roll(marks, 4, 1)
        subs = lax.broadcasted_iota(jnp.int32, (count, 8, LANES), 1)
        return jnp.where((subs >= 4) & (marks == other), -1.0, marks)

    def group_weights():
        settle(mark_a, COLS_N - 1, mark_sem.at[0, 1])
        marks = mark_a[...]
        target = marks.reshape(LANES, LANES)
        sources = voided(marks, COLS_N).reshape(LANES, LANES).T
        w_group[16:, :] = jnp.where(like & (target == sources), 1.0, 0.0).astype(bf16)
        block_first = jnp.min(jnp.min(marks, 0), 0, keepdims=True)
        block_last = jnp.max(jnp.max(marks, 0), 0, keepdims=True)
        block_mark = jnp.where(head_half, block_first, block_last)
        block_rows = jnp.where(like[:8] & (block_mark == sources[:8]), 1.0, 0.0)
        w_group[0:16, :] = jnp.concatenate([block_rows, jnp.zeros_like(block_rows)], 0).astype(bf16)
        mark_b_send[...] = block_mark
        mark_b[0] = jnp.full((8, LANES), -1.0, f32)

    def block_weights():
        settle(mark_b, ROWS_N - 1, mark_sem.at[1, 1])
        marks_b = voided(mark_b[...], ROWS_N).reshape(8 * ROWS_N, LANES)
        marks_b = jnp.concatenate(
            [marks_b, jnp.full((LANES - 8 * ROWS_N, LANES), -1.0, f32)], 0
        )
        target = mark_a[...].reshape(LANES, LANES)
        w_block[...] = jnp.where(like & (target == marks_b.T), 1.0, 0.0).astype(bf16)

    for e in range(EXCHANGES):
        recv_b[e, 0] = jnp.zeros((8, LANES), f32)

    def tile(t):
        return slice(t * LANES, (t + 1) * LANES)

    def spread_out(e, extra):
        head = acc_ref[0:8, :]
        tail = jnp.zeros_like(head)
        wide_span = jnp.broadcast_to(span[:, 0:1], (8, WIDTH))
        for k in range(1, SLOTS):
            tail = tail + jnp.where(wide_span == k, acc_ref[8 * k : 8 * k + 8, :], 0.0)
        for t in range(TILES):
            h, l = head[:, tile(t)], tail[:, tile(t)]
            send_a[e, 2 * t] = jnp.where(head_half, h, pltpu.roll(l, 4, 0))
            send_a[e, 2 * t + 1] = jnp.where(head_half, pltpu.roll(h, 4, 0), l)
        zero = jnp.zeros((8, LANES), f32)
        for m in range(2 * TILES, COLS_N):
            send_a[e, m] = zero
        if extra is not None:
            sums, counts = extra
            sub_wide = lax.broadcasted_iota(jnp.int32, (8, WIDTH), 0)
            sum_head = sums[0:1, :]
            sum_tail = jnp.sum(
                jnp.where((sub_wide == wide_span) & (sub_wide > 0), sums, 0.0), 0, keepdims=True
            )
            for t in range(TILES):
                m, r = 2 * TILES + t // 4, t % 4
                send_a[e, m, r : r + 1, :] = sum_head[:, tile(t)]
                send_a[e, m, r + 4 : r + 5, :] = sum_tail[:, tile(t)]
            count_head = counts[0:1, :]
            count_tail = jnp.sum(jnp.where((sub == span) & (sub > 0), counts, 0.0), 0, keepdims=True)
            send_a[e, 2 * TILES + 2] = jnp.where(
                head_half,
                jnp.broadcast_to(count_head, (8, LANES)),
                jnp.broadcast_to(count_tail, (8, LANES)),
            )

    def exchange(e):
        recv_a[e, 0] = send_a[e, col]
        to_cols(
            lambda o: send_a.at[e, col_at(o)],
            lambda o: recv_a.at[e, o],
            sem_a.at[e],
        )
        if e == 0:
            group_weights()
        settle(recv_a.at[e], COLS_N - 1, sem_a.at[e, 1])
        parts = split3(recv_a[e].reshape(LANES, LANES))
        send_b[e] = select_sum(w_group[0:16, :], parts)[:8]
        to_rows(send_b.at[e], lambda o: recv_b.at[e, o], sem_b.at[e])
        if e == 0:
            to_rows(mark_b_send, lambda o: mark_b.at[o], mark_sem.at[1])
        group = select_sum(w_group[16:, :], parts)
        settle(recv_b.at[e], ROWS_N - 1, sem_b.at[e, 1])
        if e == 0:
            block_weights()
        blocks = recv_b[e].reshape(8 * ROWS_N, LANES)
        blocks = jnp.concatenate([blocks, jnp.zeros((LANES - 8 * ROWS_N, LANES), f32)], 0)
        whole = group + select_sum(w_block[...], split3(blocks))
        send_c[e] = whole.reshape(COLS_N, 8, LANES)
        recv_c[e, col] = send_c[e, 0]
        for o in FAR_COLS:
            pltpu.make_async_remote_copy(
                src_ref=send_c.at[e, o],
                dst_ref=recv_c.at[e, col],
                send_sem=sem_c.at[e, 0],
                recv_sem=sem_c.at[e, 1],
                device_id=(row, col_at(o, -1)),
                device_id_type=MESH,
            ).start()
        settle(recv_c.at[e], COLS_N - 1, sem_c.at[e, 1])

    def gather_in(e):
        heads, tails = [], []
        for t in range(TILES):
            a, b = recv_c[e, 2 * t], recv_c[e, 2 * t + 1]
            heads.append(jnp.where(head_half, a, pltpu.roll(b, 4, 0)))
            tails.append(jnp.where(head_half, pltpu.roll(a, 4, 0), b))
        for t in range(TILES):
            whole_ref[t, 0:8, :] = heads[t]
            for k in range(1, SLOTS):
                whole_ref[t, 8 * k : 8 * k + 8, :] = jnp.where(
                    span == k, tails[t], acc_ref[8 * k : 8 * k + 8, tile(t)]
                )

    def take(k):
        return jnp.concatenate(
            [whole_ref[t, pl.ds(k, SLOTS, stride=AXES), :] for t in range(TILES)], 1
        )

    live = sub <= span

    def orthonormal(vectors):
        centre = centre_ref[...]
        for k in range(AXES):
            vector = vectors[k]
            square = jnp.sum(vector * vector, 1, keepdims=True)
            square = jnp.where(live[:, 0:1], square, 1.0)
            inverse = 1.0 / square
            for j in range(k + 1, AXES):
                along = jnp.sum(vector * vectors[j], 1, keepdims=True) * inverse
                vectors[j] = vectors[j] - along * vector
            unit = vector * (1.0 / jnp.sqrt(square))
            for t in range(TILES):
                frame_ref[t, pl.ds(k, SLOTS, stride=AXES), :] = unit[:, tile(t)]
            offset = jnp.sum(unit * centre, 1, keepdims=True)
            offset_ref[pl.ds(k, SLOTS, stride=AXES), :] = jnp.broadcast_to(offset, (8, LANES))

    acc_ref[0:64, :] = acc_ref[0:64, :] + acc_ref[64:128, :]
    counts = jnp.broadcast_to(jnp.sum(colsum_ref[0:8, :], 1, keepdims=True), (8, LANES))
    sums = acc_ref[128:136, :]
    spread_out(0, (sums, counts))
    exchange(0)
    gather_in(0)
    heads = [recv_c[0, 2 * TILES + t // 4, t % 4 : t % 4 + 1, :] for t in range(TILES)]
    tails = [recv_c[0, 2 * TILES + t // 4, t % 4 + 4 : t % 4 + 5, :] for t in range(TILES)]
    sub_wide = lax.broadcasted_iota(jnp.int32, (8, WIDTH), 0)
    wide_span = jnp.broadcast_to(span[:, 0:1], (8, WIDTH))
    sums = jnp.where(sub_wide == wide_span, jnp.concatenate(tails, 1), sums)
    sums = jnp.where(sub_wide == 0, jnp.concatenate(heads, 1), sums)
    counts = jnp.where(sub == span, recv_c[0, 2 * TILES + 2, 4:5, :], counts)
    counts = jnp.where(sub == 0, recv_c[0, 2 * TILES + 2, 0:1, :], counts)
    counts = jnp.where(live, counts, 1.0)
    centre = sums / counts[:, 0:1]
    centre_ref[...] = centre
    base_used = base_bf.astype(f32)
    vectors = []
    for k in range(AXES):
        total = jnp.sum(sums * base_used[k : k + 1, :], 1, keepdims=True)
        vectors.append(take(k) - total * centre)
    orthonormal(vectors)

    def frame_used():
        return jnp.concatenate([frame_ref[t] for t in range(TILES)], 1).astype(bf16)

    for e in range(1, EXCHANGES):
        frame = frame_used()
        acc_ref[0:64, :] = jnp.zeros((64, WIDTH), f32)
        colsum_ref[...] = jnp.zeros_like(colsum_ref)

        @pl.loop(0, ROWS // CHUNK)
        def _(c):
            start = pl.multiple_of(c * CHUNK, CHUNK)
            x = x_ref[pl.ds(start, CHUNK), :]
            s = lax.dot_general(
                frame, xt_ref[:, pl.ds(start, CHUNK)], NN, preferred_element_type=f32
            )
            rel = rel_of(start, CHUNK)
            pieces = [
                jnp.where(
                    rel == k,
                    s[8 * k : 8 * k + 8]
                    - jnp.broadcast_to(offset_ref[8 * k : 8 * k + 8, 0:1], (8, CHUNK)),
                    0.0,
                )
                for k in range(SLOTS)
            ]
            lifted = jnp.concatenate(pieces, 0).astype(bf16)
            acc_ref[0:64, :] += lax.dot_general(lifted, x, NN, preferred_element_type=f32)
            colsum_ref[...] += lane_sum(lifted.astype(f32))

        column_sums = jnp.sum(colsum_ref[...], 1, keepdims=True)
        for k in range(SLOTS):
            acc_ref[8 * k : 8 * k + 8, :] -= column_sums[8 * k : 8 * k + 8] * centre_ref[k : k + 1, :]
        spread_out(e, None)
        exchange(e)
        gather_in(e)
        orthonormal([take(k) for k in range(AXES)])

    frame = frame_used()

    @pl.loop(0, ROWS // CHUNK)
    def _(c):
        start = pl.multiple_of(c * CHUNK, CHUNK)
        s = lax.dot_general(
            frame, xt_ref[:, pl.ds(start, CHUNK)], NN, preferred_element_type=f32
        )
        rel = rel_of(start, CHUNK)
        found = jnp.zeros((8, CHUNK), f32)
        for k in range(SLOTS):
            centred = s[8 * k : 8 * k + 8] - jnp.broadcast_to(
                offset_ref[8 * k : 8 * k + 8, 0:1], (8, CHUNK)
            )
            found = jnp.where(rel == k, centred, found)
        out_ref[:, pl.ds(start, CHUNK)] = found

    settle(mark_a, COLS_N - 1, mark_sem.at[0, 0])
    settle(mark_b, ROWS_N - 1, mark_sem.at[1, 0])
    for e in range(EXCHANGES):
        settle(recv_a.at[e], COLS_N - 1, sem_a.at[e, 0])
        settle(recv_b.at[e], ROWS_N - 1, sem_b.at[e, 0])
        settle(recv_c.at[e], COLS_N - 1, sem_c.at[e, 0])


def shards(points, node_of_row, init_axes):
    vmem = pl.BlockSpec(memory_space=pltpu.VMEM)
    DMA = pltpu.SemaphoreType.DMA
    return pl.pallas_call(
        kernel,
        out_shape=jax.ShapeDtypeStruct((AXES, ROWS), f32),
        in_specs=[pl.BlockSpec(memory_space=pl.ANY), vmem, vmem],
        out_specs=vmem,
        scratch_shapes=[
            pltpu.VMEM((ROWS, WIDTH), bf16),
            pltpu.VMEM((WIDTH, ROWS), bf16),
            pltpu.VMEM((144, WIDTH), f32),
            pltpu.VMEM((TILES, 64, LANES), f32),
            pltpu.VMEM((TILES, 64, LANES), f32),
            pltpu.VMEM((64, LANES), f32),
            pltpu.VMEM((SLOTS, WIDTH), f32),
            pltpu.VMEM((64, LANES), f32),
            pltpu.VMEM((COLS_N, 8, LANES), f32),
            pltpu.VMEM((ROWS_N, 8, LANES), f32),
            pltpu.VMEM((8, LANES), f32),
            pltpu.VMEM((144, LANES), bf16),
            pltpu.VMEM((LANES, LANES), bf16),
            pltpu.VMEM((EXCHANGES, COLS_N, 8, LANES), f32),
            pltpu.VMEM((EXCHANGES, COLS_N, 8, LANES), f32),
            pltpu.VMEM((EXCHANGES, 8, LANES), f32),
            pltpu.VMEM((EXCHANGES, ROWS_N, 8, LANES), f32),
            pltpu.VMEM((EXCHANGES, COLS_N, 8, LANES), f32),
            pltpu.VMEM((EXCHANGES, COLS_N, 8, LANES), f32),
            DMA((ROWS // LOAD,)),
            DMA((2, 2)),
            DMA((EXCHANGES, 2)),
            DMA((EXCHANGES, 2)),
            DMA((EXCHANGES, 2)),
        ],
        compiler_params=pltpu.CompilerParams(
            collective_id=0, has_side_effects=True, vmem_limit_bytes=53 * 2**20
        ),
        name="principal_axes",
    )(points, node_of_row.reshape(1, ROWS), init_axes.T)


def solution(mesh):
    return jax.shard_map(
        shards,
        mesh=mesh,
        in_specs=(P(("row", "col"), None), P(("row", "col")), P()),
        out_specs=P(None, ("row", "col")),
        check_vma=False,
    )
```

```python
import functools

import jax
import jax.numpy as jnp
from jax import lax
from jax.experimental import pallas as pl
from jax.experimental.pallas import tpu as pltpu
from jax.sharding import PartitionSpec as P

AXES = 8
SLOTS = 8
WIDTH = 768
ROWS = 8192
COLS_N = 16
ROWS_N = 8
LANES = 128
TILES = WIDTH // LANES
LOAD = 1024
FIRST = 2048
CHUNK = 4096
EXCHANGES = 3
SIDE = 4


def hops(o):
    return min(o, SIDE - o)


FAR_COLS = sorted(range(1, COLS_N), key=lambda o: -hops(o // SIDE) - hops(o % SIDE))
FAR_ROWS = sorted(range(1, ROWS_N), key=lambda o: -hops(o // 2))
f32 = jnp.float32
bf16 = jnp.bfloat16
NT = (((1,), (1,)), ((), ()))
NN = (((1,), (0,)), ((), ()))
MESH = pl.DeviceIdType.MESH


def split3(value):
    high = value.astype(bf16)
    rest = value - high.astype(f32)
    mid = rest.astype(bf16)
    low = (rest - mid.astype(f32)).astype(bf16)
    return jnp.concatenate([high, mid, low], 1)


def select_sum(weights, parts):
    parts = lax.dot_general(weights, parts, NN, preferred_element_type=f32)
    return parts[:, :LANES] + parts[:, LANES : 2 * LANES] + parts[:, 2 * LANES :]


def kernel(
    points_ref,
    node_ref,
    init_ref,
    out_ref,
    x_ref,
    xt_ref,
    acc_ref,
    whole_ref,
    frame_ref,
    offset_ref,
    centre_ref,
    colsum_ref,
    mark_a,
    mark_b,
    mark_b_send,
    w_group,
    near_own,
    cross_own,
    near_block,
    cross_block,
    near_ref,
    cross_ref,
    send_a,
    recv_a,
    send_b,
    recv_b,
    send_c,
    recv_c,
    load_sem,
    mark_sem,
    sem_a,
    sem_b,
    sem_c,
):
    row = lax.axis_index("row")
    col = lax.axis_index("col")

    def load(c):
        piece = pl.ds(c * LOAD, LOAD)
        return pltpu.make_async_copy(points_ref.at[piece, :], x_ref.at[piece, :], load_sem.at[c])

    for c in range(ROWS // LOAD):
        load(c).start()

    barrier = pltpu.get_barrier_semaphore()

    def col_at(o, sign=1):
        x = lax.rem(col // SIDE + sign * (o // SIDE) + SIDE, SIDE)
        z = lax.rem(lax.rem(col, SIDE) + sign * (o % SIDE) + SIDE, SIDE)
        return x * SIDE + z

    for o in FAR_COLS:
        pl.semaphore_signal(
            barrier, inc=1, device_id=(row, col_at(o)), device_id_type=MESH
        )

    for o in FAR_ROWS:
        pl.semaphore_signal(
            barrier, inc=1, device_id=(lax.rem(row + o, ROWS_N), col), device_id_type=MESH
        )

    def to_cols(source, target, sems):
        for o in FAR_COLS:
            pltpu.make_async_remote_copy(
                src_ref=source(o),
                dst_ref=target(o),
                send_sem=sems.at[0],
                recv_sem=sems.at[1],
                device_id=(row, col_at(o)),
                device_id_type=MESH,
            ).start()

    def to_rows(source, target, sems):
        for o in FAR_ROWS:
            pltpu.make_async_remote_copy(
                src_ref=source,
                dst_ref=target(o),
                send_sem=sems.at[0],
                recv_sem=sems.at[1],
                device_id=(lax.rem(row + o, ROWS_N), col),
                device_id_type=MESH,
            ).start()

    def settle(buffer, count, sem):
        some = buffer.at[pl.ds(1, count)]
        pltpu.make_async_copy(some, some, sem).wait()

    sub = lax.broadcasted_iota(jnp.int32, (8, LANES), 0)
    head_half = sub < 4
    first = jnp.broadcast_to(node_ref[0:1, 0:1], (8, LANES))
    last = jnp.broadcast_to(node_ref[0:1, ROWS - 1 : ROWS], (8, LANES))
    span = last - first
    mark_a[0] = jnp.where(head_half, first, last).astype(f32)

    base = init_ref[...]
    base_bf = base.astype(bf16)
    base_pad = jnp.concatenate([base_bf, jnp.zeros_like(base_bf)], 0)
    acc_ref[...] = jnp.zeros_like(acc_ref)
    colsum_ref[...] = jnp.zeros_like(colsum_ref)

    def rel_of(start, size):
        ids = node_ref[:, pl.ds(start, size)]
        return jnp.broadcast_to(ids, (8, size)) - jnp.broadcast_to(first[:, 0:1], (8, size))

    def lane_sum(value):
        total = value[:, :LANES]
        for t in range(1, value.shape[1] // LANES):
            total = total + value[:, t * LANES : (t + 1) * LANES]
        return total

    def first_pass(c, n):
        FIRST = n * LOAD
        for part in range(n):
            load(c + part).wait()
        start = pl.multiple_of(c * LOAD, LOAD)
        x = x_ref[pl.ds(start, FIRST), :]
        xt = x.T
        xt_ref[:, pl.ds(start, FIRST)] = xt
        s = lax.dot_general(base_pad, xt, NN, preferred_element_type=f32)[:8]
        high = s.astype(bf16).astype(f32)
        low = s - high
        rel = rel_of(start, FIRST)
        sub_wide = lax.broadcasted_iota(jnp.int32, (8, FIRST), 0)
        member = jnp.where(rel == sub_wide, 1.0, 0.0)
        pieces = [jnp.where(rel == k, high, 0.0) for k in range(SLOTS)]
        pieces += [jnp.where(rel == k, low, 0.0) for k in range(SLOTS)]
        pieces += [member, jnp.zeros_like(member)]
        lifted = jnp.concatenate(pieces, 0).astype(bf16)
        acc_ref[...] += lax.dot_general(lifted, x, NN, preferred_element_type=f32)
        colsum_ref[0:8, :] += lane_sum(member)

    def first_range(lower, upper):
        first_pass(0, 1)
        first_pass(1, 1)

        @pl.loop(1, 4)
        def _(c):
            first_pass(2 * c, 2)

    first_range(0, ROWS // FIRST)
    pl.semaphore_wait(barrier, COLS_N - 1 + ROWS_N - 1)
    to_cols(lambda o: mark_a.at[0], lambda o: mark_a.at[o], mark_sem.at[0])
    like = (
        lax.rem(lax.broadcasted_iota(jnp.int32, (LANES, LANES), 0), 4)
        == lax.rem(lax.broadcasted_iota(jnp.int32, (LANES, LANES), 1), 4)
    )

    def voided(marks, count):
        other = pltpu.roll(marks, 4, 1)
        subs = lax.broadcasted_iota(jnp.int32, (count, 8, LANES), 1)
        return jnp.where((subs >= 4) & (marks == other), -1.0, marks)

    def group_weights():
        settle(mark_a, COLS_N - 1, mark_sem.at[0, 1])
        marks = mark_a[...]
        target = marks.reshape(LANES, LANES)
        sources = voided(marks, COLS_N).reshape(LANES, LANES).T
        w_group[...] = jnp.where(like & (target == sources), 1.0, 0.0).astype(bf16)
        block_first = jnp.min(jnp.min(marks, 0), 0, keepdims=True)
        block_last = jnp.max(jnp.max(marks, 0), 0, keepdims=True)
        block_mark = jnp.where(head_half, block_first, block_last)
        usable = voided(marks, COLS_N)
        wide = jnp.broadcast_to(block_mark[None], (COLS_N, 8, LANES))
        other = pltpu.roll(block_mark, 4, 0)
        near_own[...] = jnp.where(marks == wide, 1.0, 0.0)
        cross_own[...] = jnp.where(
            (marks == jnp.broadcast_to(other[None], marks.shape))
            & jnp.broadcast_to((other != block_mark)[None], marks.shape),
            1.0,
            0.0,
        )
        near_ref[...] = jnp.where(usable == wide, 1.0, 0.0)
        cross_ref[...] = jnp.where(pltpu.roll(usable, 4, 1) == wide, 1.0, 0.0)
        mark_b_send[...] = block_mark
        mark_b[0] = jnp.full((8, LANES), -1.0, f32)

    def block_weights():
        settle(mark_b, ROWS_N - 1, mark_sem.at[1, 1])
        usable = voided(mark_b[...], ROWS_N)
        wide = jnp.broadcast_to(mark_b_send[...][None], (ROWS_N, 8, LANES))
        near_block[...] = jnp.where(usable == wide, 1.0, 0.0)
        cross_block[...] = jnp.where(pltpu.roll(usable, 4, 1) == wide, 1.0, 0.0)

    for e in range(EXCHANGES):
        recv_b[e, 0] = jnp.zeros((8, LANES), f32)

    def tile(t):
        return slice(t * LANES, (t + 1) * LANES)

    def spread_out(e, extra):
        head = acc_ref[0:8, :]
        tail = jnp.zeros_like(head)
        wide_span = jnp.broadcast_to(span[:, 0:1], (8, WIDTH))
        for k in range(1, SLOTS):
            tail = tail + jnp.where(wide_span == k, acc_ref[8 * k : 8 * k + 8, :], 0.0)
        for t in range(TILES):
            h, l = head[:, tile(t)], tail[:, tile(t)]
            send_a[e, 2 * t] = jnp.where(head_half, h, pltpu.roll(l, 4, 0))
            send_a[e, 2 * t + 1] = jnp.where(head_half, pltpu.roll(h, 4, 0), l)
        zero = jnp.zeros((8, LANES), f32)
        for m in range(2 * TILES, COLS_N):
            send_a[e, m] = zero
        if extra is not None:
            sums, counts = extra
            sub_wide = lax.broadcasted_iota(jnp.int32, (8, WIDTH), 0)
            sum_head = sums[0:1, :]
            sum_tail = jnp.sum(
                jnp.where((sub_wide == wide_span) & (sub_wide > 0), sums, 0.0), 0, keepdims=True
            )
            for t in range(TILES):
                m, r = 2 * TILES + t // 4, t % 4
                send_a[e, m, r : r + 1, :] = sum_head[:, tile(t)]
                send_a[e, m, r + 4 : r + 5, :] = sum_tail[:, tile(t)]
            count_head = counts[0:1, :]
            count_tail = jnp.sum(jnp.where((sub == span) & (sub > 0), counts, 0.0), 0, keepdims=True)
            send_a[e, 2 * TILES + 2] = jnp.where(
                head_half,
                jnp.broadcast_to(count_head, (8, LANES)),
                jnp.broadcast_to(count_tail, (8, LANES)),
            )

    def exchange(e):
        recv_a[e, 0] = send_a[e, col]
        to_cols(
            lambda o: send_a.at[e, col_at(o)],
            lambda o: recv_a.at[e, o],
            sem_a.at[e],
        )
        if e == 0:
            group_weights()
        settle(recv_a.at[e], COLS_N - 1, sem_a.at[e, 1])
        tiles = recv_a[e]
        send_b[e] = jnp.sum(near_ref[...] * tiles, 0) + jnp.sum(
            cross_ref[...] * pltpu.roll(tiles, 4, 1), 0
        )
        to_rows(send_b.at[e], lambda o: recv_b.at[e, o], sem_b.at[e])
        if e == 0:
            to_rows(mark_b_send, lambda o: mark_b.at[o], mark_sem.at[1])
        group = select_sum(w_group[...], split3(tiles.reshape(LANES, LANES)))
        settle(recv_b.at[e], ROWS_N - 1, sem_b.at[e, 1])
        if e == 0:
            block_weights()
        blocks = recv_b[e]
        outer = jnp.sum(near_block[...] * blocks, 0) + jnp.sum(
            cross_block[...] * pltpu.roll(blocks, 4, 1), 0
        )
        send_c[e] = (
            group.reshape(COLS_N, 8, LANES)
            + near_own[...] * outer[None]
            + cross_own[...] * pltpu.roll(outer, 4, 0)[None]
        )
        recv_c[e, col] = send_c[e, 0]
        for o in FAR_COLS:
            pltpu.make_async_remote_copy(
                src_ref=send_c.at[e, o],
                dst_ref=recv_c.at[e, col],
                send_sem=sem_c.at[e, 0],
                recv_sem=sem_c.at[e, 1],
                device_id=(row, col_at(o, -1)),
                device_id_type=MESH,
            ).start()
        settle(recv_c.at[e], COLS_N - 1, sem_c.at[e, 1])

    def gather_in(e):
        heads, tails = [], []
        for t in range(TILES):
            a, b = recv_c[e, 2 * t], recv_c[e, 2 * t + 1]
            heads.append(jnp.where(head_half, a, pltpu.roll(b, 4, 0)))
            tails.append(jnp.where(head_half, pltpu.roll(a, 4, 0), b))
        for t in range(TILES):
            whole_ref[t, 0:8, :] = heads[t]
            for k in range(1, SLOTS):
                whole_ref[t, 8 * k : 8 * k + 8, :] = jnp.where(
                    span == k, tails[t], acc_ref[8 * k : 8 * k + 8, tile(t)]
                )

    def take(k):
        return jnp.concatenate(
            [whole_ref[t, pl.ds(k, SLOTS, stride=AXES), :] for t in range(TILES)], 1
        )

    live = sub <= span

    def orthonormal(vectors):
        centre = centre_ref[...]
        for k in range(AXES):
            vector = vectors[k]
            square = jnp.sum(vector * vector, 1, keepdims=True)
            square = jnp.where(live[:, 0:1], square, 1.0)
            inverse = 1.0 / square
            for j in range(k + 1, AXES):
                along = jnp.sum(vector * vectors[j], 1, keepdims=True) * inverse
                vectors[j] = vectors[j] - along * vector
            unit = vector * (1.0 / jnp.sqrt(square))
            for t in range(TILES):
                frame_ref[t, pl.ds(k, SLOTS, stride=AXES), :] = unit[:, tile(t)]
            offset = jnp.sum(unit * centre, 1, keepdims=True)
            offset_ref[pl.ds(k, SLOTS, stride=AXES), :] = jnp.broadcast_to(offset, (8, LANES))

    acc_ref[0:64, :] = acc_ref[0:64, :] + acc_ref[64:128, :]
    counts = jnp.broadcast_to(jnp.sum(colsum_ref[0:8, :], 1, keepdims=True), (8, LANES))
    sums = acc_ref[128:136, :]
    spread_out(0, (sums, counts))
    exchange(0)
    gather_in(0)
    heads = [recv_c[0, 2 * TILES + t // 4, t % 4 : t % 4 + 1, :] for t in range(TILES)]
    tails = [recv_c[0, 2 * TILES + t // 4, t % 4 + 4 : t % 4 + 5, :] for t in range(TILES)]
    sub_wide = lax.broadcasted_iota(jnp.int32, (8, WIDTH), 0)
    wide_span = jnp.broadcast_to(span[:, 0:1], (8, WIDTH))
    sums = jnp.where(sub_wide == wide_span, jnp.concatenate(tails, 1), sums)
    sums = jnp.where(sub_wide == 0, jnp.concatenate(heads, 1), sums)
    counts = jnp.where(sub == span, recv_c[0, 2 * TILES + 2, 4:5, :], counts)
    counts = jnp.where(sub == 0, recv_c[0, 2 * TILES + 2, 0:1, :], counts)
    counts = jnp.where(live, counts, 1.0)
    centre = sums / counts[:, 0:1]
    centre_ref[...] = centre
    base_used = base_bf.astype(f32)
    vectors = []
    for k in range(AXES):
        total = jnp.sum(sums * base_used[k : k + 1, :], 1, keepdims=True)
        vectors.append(take(k) - total * centre)
    orthonormal(vectors)

    def frame_used():
        return jnp.concatenate([frame_ref[t] for t in range(TILES)], 1).astype(bf16)

    for e in range(1, EXCHANGES):
        frame = frame_used()
        acc_ref[0:64, :] = jnp.zeros((64, WIDTH), f32)
        colsum_ref[...] = jnp.zeros_like(colsum_ref)

        @pl.loop(0, ROWS // CHUNK)
        def _(c):
            start = pl.multiple_of(c * CHUNK, CHUNK)
            x = x_ref[pl.ds(start, CHUNK), :]
            s = lax.dot_general(
                frame, xt_ref[:, pl.ds(start, CHUNK)], NN, preferred_element_type=f32
            )
            rel = rel_of(start, CHUNK)
            pieces = [
                jnp.where(
                    rel == k,
                    s[8 * k : 8 * k + 8]
                    - jnp.broadcast_to(offset_ref[8 * k : 8 * k + 8, 0:1], (8, CHUNK)),
                    0.0,
                )
                for k in range(SLOTS)
            ]
            lifted = jnp.concatenate(pieces, 0).astype(bf16)
            acc_ref[0:64, :] += lax.dot_general(lifted, x, NN, preferred_element_type=f32)
            colsum_ref[...] += lane_sum(lifted.astype(f32))

        column_sums = jnp.sum(colsum_ref[...], 1, keepdims=True)
        for k in range(SLOTS):
            acc_ref[8 * k : 8 * k + 8, :] -= column_sums[8 * k : 8 * k + 8] * centre_ref[k : k + 1, :]
        spread_out(e, None)
        exchange(e)
        gather_in(e)
        orthonormal([take(k) for k in range(AXES)])

    frame = frame_used()

    @pl.loop(0, 1)
    def _(c):
        start = pl.multiple_of(c * ROWS, ROWS)
        s = lax.dot_general(
            frame, xt_ref[:, pl.ds(start, ROWS)], NN, preferred_element_type=f32
        )
        rel = rel_of(start, ROWS)
        found = jnp.zeros((8, ROWS), f32)
        for k in range(SLOTS):
            centred = s[8 * k : 8 * k + 8] - jnp.broadcast_to(
                offset_ref[8 * k : 8 * k + 8, 0:1], (8, ROWS)
            )
            found = jnp.where(rel == k, centred, found)
        out_ref[:, pl.ds(start, ROWS)] = found

    settle(mark_a, COLS_N - 1, mark_sem.at[0, 0])
    settle(mark_b, ROWS_N - 1, mark_sem.at[1, 0])
    for e in range(EXCHANGES):
        settle(recv_a.at[e], COLS_N - 1, sem_a.at[e, 0])
        settle(recv_b.at[e], ROWS_N - 1, sem_b.at[e, 0])
        settle(recv_c.at[e], COLS_N - 1, sem_c.at[e, 0])


def shards(points, node_of_row, init_axes):
    vmem = pl.BlockSpec(memory_space=pltpu.VMEM)
    DMA = pltpu.SemaphoreType.DMA
    return pl.pallas_call(
        kernel,
        out_shape=jax.ShapeDtypeStruct((AXES, ROWS), f32),
        in_specs=[pl.BlockSpec(memory_space=pl.ANY), vmem, vmem],
        out_specs=vmem,
        scratch_shapes=[
            pltpu.VMEM((ROWS, WIDTH), bf16),
            pltpu.VMEM((WIDTH, ROWS), bf16),
            pltpu.VMEM((144, WIDTH), f32),
            pltpu.VMEM((TILES, 64, LANES), f32),
            pltpu.VMEM((TILES, 64, LANES), f32),
            pltpu.VMEM((64, LANES), f32),
            pltpu.VMEM((SLOTS, WIDTH), f32),
            pltpu.VMEM((64, LANES), f32),
            pltpu.VMEM((COLS_N, 8, LANES), f32),
            pltpu.VMEM((ROWS_N, 8, LANES), f32),
            pltpu.VMEM((8, LANES), f32),
            pltpu.VMEM((LANES, LANES), bf16),
            pltpu.VMEM((COLS_N, 8, LANES), f32),
            pltpu.VMEM((COLS_N, 8, LANES), f32),
            pltpu.VMEM((ROWS_N, 8, LANES), f32),
            pltpu.VMEM((ROWS_N, 8, LANES), f32),
            pltpu.VMEM((COLS_N, 8, LANES), f32),
            pltpu.VMEM((COLS_N, 8, LANES), f32),
            pltpu.VMEM((EXCHANGES, COLS_N, 8, LANES), f32),
            pltpu.VMEM((EXCHANGES, COLS_N, 8, LANES), f32),
            pltpu.VMEM((EXCHANGES, 8, LANES), f32),
            pltpu.VMEM((EXCHANGES, ROWS_N, 8, LANES), f32),
            pltpu.VMEM((EXCHANGES, COLS_N, 8, LANES), f32),
            pltpu.VMEM((EXCHANGES, COLS_N, 8, LANES), f32),
            DMA((ROWS // LOAD,)),
            DMA((2, 2)),
            DMA((EXCHANGES, 2)),
            DMA((EXCHANGES, 2)),
            DMA((EXCHANGES, 2)),
        ],
        compiler_params=pltpu.CompilerParams(
            collective_id=0, has_side_effects=True, vmem_limit_bytes=53 * 2**20
        ),
        name="principal_axes",
    )(points, node_of_row.reshape(1, ROWS), init_axes.T)


def solution(mesh):
    return jax.shard_map(
        shards,
        mesh=mesh,
        in_specs=(P(("row", "col"), None), P(("row", "col")), P()),
        out_specs=P(None, ("row", "col")),
        check_vma=False,
    )
```

```python
import functools

import jax
import jax.numpy as jnp
from jax import lax
from jax.experimental import pallas as pl
from jax.experimental.pallas import tpu as pltpu
from jax.sharding import PartitionSpec as P

AXES = 8
SLOTS = 8
WIDTH = 768
ROWS = 8192
COLS_N = 16
ROWS_N = 8
LANES = 128
TILES = WIDTH // LANES
LOAD = 1024
FIRST = 2048
CHUNK = 4096
EXCHANGES = 3
SIDE = 4


def hops(o):
    return min(o, SIDE - o)


FAR_COLS = sorted(range(1, COLS_N), key=lambda o: -hops(o // SIDE) - hops(o % SIDE))
FAR_ROWS = sorted(range(1, ROWS_N), key=lambda o: -hops(o // 2))
f32 = jnp.float32
bf16 = jnp.bfloat16
NT = (((1,), (1,)), ((), ()))
NN = (((1,), (0,)), ((), ()))
MESH = pl.DeviceIdType.MESH


def split3(value):
    high = value.astype(bf16)
    rest = value - high.astype(f32)
    mid = rest.astype(bf16)
    low = (rest - mid.astype(f32)).astype(bf16)
    return jnp.concatenate([high, mid, low], 1)


def select_sum(weights, parts):
    parts = lax.dot_general(weights, parts, NN, preferred_element_type=f32)
    return parts[:, :LANES] + parts[:, LANES : 2 * LANES] + parts[:, 2 * LANES :]


def kernel(
    points_ref,
    node_ref,
    init_ref,
    out_ref,
    x_ref,
    xt_ref,
    acc_ref,
    whole_ref,
    frame_ref,
    offset_ref,
    centre_ref,
    colsum_ref,
    mark_a,
    mark_b,
    mark_b_send,
    w_group,
    near_own,
    cross_own,
    near_block,
    cross_block,
    near_ref,
    cross_ref,
    send_a,
    recv_a,
    send_b,
    recv_b,
    send_c,
    recv_c,
    load_sem,
    mark_sem,
    sem_a,
    sem_b,
    sem_c,
):
    row = lax.axis_index("row")
    col = lax.axis_index("col")

    def load(c):
        piece = pl.ds(c * LOAD, LOAD)
        return pltpu.make_async_copy(points_ref.at[piece, :], x_ref.at[piece, :], load_sem.at[c])

    for c in range(ROWS // LOAD):
        load(c).start()

    barrier = pltpu.get_barrier_semaphore()

    def col_at(o, sign=1):
        x = lax.rem(col // SIDE + sign * (o // SIDE) + SIDE, SIDE)
        z = lax.rem(lax.rem(col, SIDE) + sign * (o % SIDE) + SIDE, SIDE)
        return x * SIDE + z

    for o in FAR_COLS:
        pl.semaphore_signal(
            barrier, inc=1, device_id=(row, col_at(o)), device_id_type=MESH
        )

    for o in FAR_ROWS:
        pl.semaphore_signal(
            barrier, inc=1, device_id=(lax.rem(row + o, ROWS_N), col), device_id_type=MESH
        )

    def to_cols(source, target, sems):
        for o in FAR_COLS:
            pltpu.make_async_remote_copy(
                src_ref=source(o),
                dst_ref=target(o),
                send_sem=sems.at[0],
                recv_sem=sems.at[1],
                device_id=(row, col_at(o)),
                device_id_type=MESH,
            ).start()

    def to_rows(source, target, sems):
        for o in FAR_ROWS:
            pltpu.make_async_remote_copy(
                src_ref=source,
                dst_ref=target(o),
                send_sem=sems.at[0],
                recv_sem=sems.at[1],
                device_id=(lax.rem(row + o, ROWS_N), col),
                device_id_type=MESH,
            ).start()

    def settle(buffer, count, sem):
        some = buffer.at[pl.ds(1, count)]
        pltpu.make_async_copy(some, some, sem).wait()

    sub = lax.broadcasted_iota(jnp.int32, (8, LANES), 0)
    head_half = sub < 4
    first = jnp.broadcast_to(node_ref[0:1, 0:1], (8, LANES))
    last = jnp.broadcast_to(node_ref[0:1, ROWS - 1 : ROWS], (8, LANES))
    span = last - first
    mark_a[0] = jnp.where(head_half, first, last).astype(f32)

    base = init_ref[...]
    base_bf = base.astype(bf16)
    base_pad = jnp.concatenate([base_bf, jnp.zeros_like(base_bf)], 0)
    acc_ref[...] = jnp.zeros_like(acc_ref)
    colsum_ref[...] = jnp.zeros_like(colsum_ref)

    def rel_of(start, size):
        ids = node_ref[:, pl.ds(start, size)]
        return jnp.broadcast_to(ids, (8, size)) - jnp.broadcast_to(first[:, 0:1], (8, size))

    def lane_sum(value):
        total = value[:, :LANES]
        for t in range(1, value.shape[1] // LANES):
            total = total + value[:, t * LANES : (t + 1) * LANES]
        return total

    def first_pass(c, n):
        FIRST = n * LOAD
        for part in range(n):
            load(c + part).wait()
        start = pl.multiple_of(c * LOAD, LOAD)
        x = x_ref[pl.ds(start, FIRST), :]
        xt = x.T
        xt_ref[:, pl.ds(start, FIRST)] = xt
        s = lax.dot_general(base_pad, xt, NN, preferred_element_type=f32)[:8]
        high = s.astype(bf16).astype(f32)
        low = s - high
        rel = rel_of(start, FIRST)
        sub_wide = lax.broadcasted_iota(jnp.int32, (8, FIRST), 0)
        member = jnp.where(rel == sub_wide, 1.0, 0.0)
        pieces = [jnp.where(rel == k, high, 0.0) for k in range(SLOTS)]
        pieces += [jnp.where(rel == k, low, 0.0) for k in range(SLOTS)]
        pieces += [member, jnp.zeros_like(member)]
        lifted = jnp.concatenate(pieces, 0).astype(bf16)
        acc_ref[...] += lax.dot_general(lifted, x, NN, preferred_element_type=f32)
        colsum_ref[0:8, :] += lane_sum(member)

    def first_range(lower, upper):
        first_pass(0, 1)
        first_pass(1, 1)

        @pl.loop(1, 3)
        def _(c):
            first_pass(2 * c, 2)

    first_range(0, ROWS // FIRST)
    pl.semaphore_wait(barrier, COLS_N - 1 + ROWS_N - 1)
    to_cols(lambda o: mark_a.at[0], lambda o: mark_a.at[o], mark_sem.at[0])

    @pl.loop(3, 4)
    def _(c):
        first_pass(2 * c, 2)

    like = (
        lax.rem(lax.broadcasted_iota(jnp.int32, (LANES, LANES), 0), 4)
        == lax.rem(lax.broadcasted_iota(jnp.int32, (LANES, LANES), 1), 4)
    )

    def voided(marks, count):
        other = pltpu.roll(marks, 4, 1)
        subs = lax.broadcasted_iota(jnp.int32, (count, 8, LANES), 1)
        return jnp.where((subs >= 4) & (marks == other), -1.0, marks)

    def group_weights():
        settle(mark_a, COLS_N - 1, mark_sem.at[0, 1])
        marks = mark_a[...]
        target = marks.reshape(LANES, LANES)
        sources = voided(marks, COLS_N).reshape(LANES, LANES).T
        w_group[...] = jnp.where(like & (target == sources), 1.0, 0.0).astype(bf16)
        block_first = jnp.min(jnp.min(marks, 0), 0, keepdims=True)
        block_last = jnp.max(jnp.max(marks, 0), 0, keepdims=True)
        block_mark = jnp.where(head_half, block_first, block_last)
        usable = voided(marks, COLS_N)
        wide = jnp.broadcast_to(block_mark[None], (COLS_N, 8, LANES))
        other = pltpu.roll(block_mark, 4, 0)
        near_own[...] = jnp.where(marks == wide, 1.0, 0.0)
        cross_own[...] = jnp.where(
            (marks == jnp.broadcast_to(other[None], marks.shape))
            & jnp.broadcast_to((other != block_mark)[None], marks.shape),
            1.0,
            0.0,
        )
        near_ref[...] = jnp.where(usable == wide, 1.0, 0.0)
        cross_ref[...] = jnp.where(pltpu.roll(usable, 4, 1) == wide, 1.0, 0.0)
        mark_b_send[...] = block_mark
        mark_b[0] = jnp.full((8, LANES), -1.0, f32)

    def block_weights():
        settle(mark_b, ROWS_N - 1, mark_sem.at[1, 1])
        usable = voided(mark_b[...], ROWS_N)
        wide = jnp.broadcast_to(mark_b_send[...][None], (ROWS_N, 8, LANES))
        near_block[...] = jnp.where(usable == wide, 1.0, 0.0)
        cross_block[...] = jnp.where(pltpu.roll(usable, 4, 1) == wide, 1.0, 0.0)

    for e in range(EXCHANGES):
        recv_b[e, 0] = jnp.zeros((8, LANES), f32)

    def tile(t):
        return slice(t * LANES, (t + 1) * LANES)

    def spread_out(e, extra):
        head = acc_ref[0:8, :]
        tail = jnp.zeros_like(head)
        wide_span = jnp.broadcast_to(span[:, 0:1], (8, WIDTH))
        for k in range(1, SLOTS):
            tail = tail + jnp.where(wide_span == k, acc_ref[8 * k : 8 * k + 8, :], 0.0)
        for t in range(TILES):
            h, l = head[:, tile(t)], tail[:, tile(t)]
            send_a[e, 2 * t] = jnp.where(head_half, h, pltpu.roll(l, 4, 0))
            send_a[e, 2 * t + 1] = jnp.where(head_half, pltpu.roll(h, 4, 0), l)
        zero = jnp.zeros((8, LANES), f32)
        for m in range(2 * TILES, COLS_N):
            send_a[e, m] = zero
        if extra is not None:
            sums, counts = extra
            sub_wide = lax.broadcasted_iota(jnp.int32, (8, WIDTH), 0)
            sum_head = sums[0:1, :]
            sum_tail = jnp.sum(
                jnp.where((sub_wide == wide_span) & (sub_wide > 0), sums, 0.0), 0, keepdims=True
            )
            for t in range(TILES):
                m, r = 2 * TILES + t // 4, t % 4
                send_a[e, m, r : r + 1, :] = sum_head[:, tile(t)]
                send_a[e, m, r + 4 : r + 5, :] = sum_tail[:, tile(t)]
            count_head = counts[0:1, :]
            count_tail = jnp.sum(jnp.where((sub == span) & (sub > 0), counts, 0.0), 0, keepdims=True)
            send_a[e, 2 * TILES + 2] = jnp.where(
                head_half,
                jnp.broadcast_to(count_head, (8, LANES)),
                jnp.broadcast_to(count_tail, (8, LANES)),
            )

    def exchange(e):
        recv_a[e, 0] = send_a[e, col]
        to_cols(
            lambda o: send_a.at[e, col_at(o)],
            lambda o: recv_a.at[e, o],
            sem_a.at[e],
        )
        if e == 0:
            group_weights()
        settle(recv_a.at[e], COLS_N - 1, sem_a.at[e, 1])
        tiles = recv_a[e]
        send_b[e] = jnp.sum(near_ref[...] * tiles, 0) + jnp.sum(
            cross_ref[...] * pltpu.roll(tiles, 4, 1), 0
        )
        to_rows(send_b.at[e], lambda o: recv_b.at[e, o], sem_b.at[e])
        if e == 0:
            to_rows(mark_b_send, lambda o: mark_b.at[o], mark_sem.at[1])
        group = select_sum(w_group[...], split3(tiles.reshape(LANES, LANES)))
        settle(recv_b.at[e], ROWS_N - 1, sem_b.at[e, 1])
        if e == 0:
            block_weights()
        blocks = recv_b[e]
        outer = jnp.sum(near_block[...] * blocks, 0) + jnp.sum(
            cross_block[...] * pltpu.roll(blocks, 4, 1), 0
        )
        send_c[e] = (
            group.reshape(COLS_N, 8, LANES)
            + near_own[...] * outer[None]
            + cross_own[...] * pltpu.roll(outer, 4, 0)[None]
        )
        recv_c[e, col] = send_c[e, 0]
        for o in FAR_COLS:
            pltpu.make_async_remote_copy(
                src_ref=send_c.at[e, o],
                dst_ref=recv_c.at[e, col],
                send_sem=sem_c.at[e, 0],
                recv_sem=sem_c.at[e, 1],
                device_id=(row, col_at(o, -1)),
                device_id_type=MESH,
            ).start()
        settle(recv_c.at[e], COLS_N - 1, sem_c.at[e, 1])

    def gather_in(e):
        heads, tails = [], []
        for t in range(TILES):
            a, b = recv_c[e, 2 * t], recv_c[e, 2 * t + 1]
            heads.append(jnp.where(head_half, a, pltpu.roll(b, 4, 0)))
            tails.append(jnp.where(head_half, pltpu.roll(a, 4, 0), b))
        for t in range(TILES):
            whole_ref[t, 0:8, :] = heads[t]
            for k in range(1, SLOTS):
                whole_ref[t, 8 * k : 8 * k + 8, :] = jnp.where(
                    span == k, tails[t], acc_ref[8 * k : 8 * k + 8, tile(t)]
                )

    def take(k):
        return jnp.concatenate(
            [whole_ref[t, pl.ds(k, SLOTS, stride=AXES), :] for t in range(TILES)], 1
        )

    live = sub <= span

    def orthonormal(vectors):
        centre = centre_ref[...]
        for k in range(AXES):
            vector = vectors[k]
            square = jnp.sum(vector * vector, 1, keepdims=True)
            square = jnp.where(live[:, 0:1], square, 1.0)
            inverse = pl.reciprocal(square)
            for j in range(k + 1, AXES):
                along = jnp.sum(vector * vectors[j], 1, keepdims=True) * inverse
                vectors[j] = vectors[j] - along * vector
            unit = vector * (1.0 / jnp.sqrt(square))
            for t in range(TILES):
                frame_ref[t, pl.ds(k, SLOTS, stride=AXES), :] = unit[:, tile(t)]
            offset = jnp.sum(unit * centre, 1, keepdims=True)
            offset_ref[pl.ds(k, SLOTS, stride=AXES), :] = jnp.broadcast_to(offset, (8, LANES))

    acc_ref[0:64, :] = acc_ref[0:64, :] + acc_ref[64:128, :]
    counts = jnp.broadcast_to(jnp.sum(colsum_ref[0:8, :], 1, keepdims=True), (8, LANES))
    sums = acc_ref[128:136, :]
    spread_out(0, (sums, counts))
    exchange(0)
    gather_in(0)
    heads = [recv_c[0, 2 * TILES + t // 4, t % 4 : t % 4 + 1, :] for t in range(TILES)]
    tails = [recv_c[0, 2 * TILES + t // 4, t % 4 + 4 : t % 4 + 5, :] for t in range(TILES)]
    sub_wide = lax.broadcasted_iota(jnp.int32, (8, WIDTH), 0)
    wide_span = jnp.broadcast_to(span[:, 0:1], (8, WIDTH))
    sums = jnp.where(sub_wide == wide_span, jnp.concatenate(tails, 1), sums)
    sums = jnp.where(sub_wide == 0, jnp.concatenate(heads, 1), sums)
    counts = jnp.where(sub == span, recv_c[0, 2 * TILES + 2, 4:5, :], counts)
    counts = jnp.where(sub == 0, recv_c[0, 2 * TILES + 2, 0:1, :], counts)
    counts = jnp.where(live, counts, 1.0)
    centre = sums / counts[:, 0:1]
    centre_ref[...] = centre
    base_used = base_bf.astype(f32)
    vectors = []
    for k in range(AXES):
        total = jnp.sum(sums * base_used[k : k + 1, :], 1, keepdims=True)
        vectors.append(take(k) - total * centre)
    orthonormal(vectors)

    def frame_used():
        return jnp.concatenate([frame_ref[t] for t in range(TILES)], 1).astype(bf16)

    for e in range(1, EXCHANGES):
        frame = frame_used()
        acc_ref[0:64, :] = jnp.zeros((64, WIDTH), f32)
        colsum_ref[...] = jnp.zeros_like(colsum_ref)

        @pl.loop(0, ROWS // CHUNK)
        def _(c):
            start = pl.multiple_of(c * CHUNK, CHUNK)
            x = x_ref[pl.ds(start, CHUNK), :]
            s = lax.dot_general(
                frame, xt_ref[:, pl.ds(start, CHUNK)], NN, preferred_element_type=f32
            )
            rel = rel_of(start, CHUNK)
            pieces = [
                jnp.where(
                    rel == k,
                    s[8 * k : 8 * k + 8]
                    - jnp.broadcast_to(offset_ref[8 * k : 8 * k + 8, 0:1], (8, CHUNK)),
                    0.0,
                )
                for k in range(SLOTS)
            ]
            lifted = jnp.concatenate(pieces, 0).astype(bf16)
            acc_ref[0:64, :] += lax.dot_general(lifted, x, NN, preferred_element_type=f32)
            colsum_ref[...] += lane_sum(lifted.astype(f32))

        column_sums = jnp.sum(colsum_ref[...], 1, keepdims=True)
        for k in range(SLOTS):
            acc_ref[8 * k : 8 * k + 8, :] -= column_sums[8 * k : 8 * k + 8] * centre_ref[k : k + 1, :]
        spread_out(e, None)
        exchange(e)
        gather_in(e)
        orthonormal([take(k) for k in range(AXES)])

    frame = frame_used()

    @pl.loop(0, 1)
    def _(c):
        start = pl.multiple_of(c * ROWS, ROWS)
        s = lax.dot_general(
            frame, xt_ref[:, pl.ds(start, ROWS)], NN, preferred_element_type=f32
        )
        rel = rel_of(start, ROWS)
        found = jnp.zeros((8, ROWS), f32)
        for k in range(SLOTS):
            centred = s[8 * k : 8 * k + 8] - jnp.broadcast_to(
                offset_ref[8 * k : 8 * k + 8, 0:1], (8, ROWS)
            )
            found = jnp.where(rel == k, centred, found)
        out_ref[:, pl.ds(start, ROWS)] = found

    settle(mark_a, COLS_N - 1, mark_sem.at[0, 0])
    settle(mark_b, ROWS_N - 1, mark_sem.at[1, 0])
    for e in range(EXCHANGES):
        settle(recv_a.at[e], COLS_N - 1, sem_a.at[e, 0])
        settle(recv_b.at[e], ROWS_N - 1, sem_b.at[e, 0])
        settle(recv_c.at[e], COLS_N - 1, sem_c.at[e, 0])


def shards(points, node_of_row, init_axes):
    vmem = pl.BlockSpec(memory_space=pltpu.VMEM)
    DMA = pltpu.SemaphoreType.DMA
    return pl.pallas_call(
        kernel,
        out_shape=jax.ShapeDtypeStruct((AXES, ROWS), f32),
        in_specs=[pl.BlockSpec(memory_space=pl.ANY), vmem, vmem],
        out_specs=vmem,
        scratch_shapes=[
            pltpu.VMEM((ROWS, WIDTH), bf16),
            pltpu.VMEM((WIDTH, ROWS), bf16),
            pltpu.VMEM((144, WIDTH), f32),
            pltpu.VMEM((TILES, 64, LANES), f32),
            pltpu.VMEM((TILES, 64, LANES), f32),
            pltpu.VMEM((64, LANES), f32),
            pltpu.VMEM((SLOTS, WIDTH), f32),
            pltpu.VMEM((64, LANES), f32),
            pltpu.VMEM((COLS_N, 8, LANES), f32),
            pltpu.VMEM((ROWS_N, 8, LANES), f32),
            pltpu.VMEM((8, LANES), f32),
            pltpu.VMEM((LANES, LANES), bf16),
            pltpu.VMEM((COLS_N, 8, LANES), f32),
            pltpu.VMEM((COLS_N, 8, LANES), f32),
            pltpu.VMEM((ROWS_N, 8, LANES), f32),
            pltpu.VMEM((ROWS_N, 8, LANES), f32),
            pltpu.VMEM((COLS_N, 8, LANES), f32),
            pltpu.VMEM((COLS_N, 8, LANES), f32),
            pltpu.VMEM((EXCHANGES, COLS_N, 8, LANES), f32),
            pltpu.VMEM((EXCHANGES, COLS_N, 8, LANES), f32),
            pltpu.VMEM((EXCHANGES, 8, LANES), f32),
            pltpu.VMEM((EXCHANGES, ROWS_N, 8, LANES), f32),
            pltpu.VMEM((EXCHANGES, COLS_N, 8, LANES), f32),
            pltpu.VMEM((EXCHANGES, COLS_N, 8, LANES), f32),
            DMA((ROWS // LOAD,)),
            DMA((2, 2)),
            DMA((EXCHANGES, 2)),
            DMA((EXCHANGES, 2)),
            DMA((EXCHANGES, 2)),
        ],
        compiler_params=pltpu.CompilerParams(
            collective_id=0, has_side_effects=True, vmem_limit_bytes=53 * 2**20
        ),
        name="principal_axes",
    )(points, node_of_row.reshape(1, ROWS), init_axes.T)


def solution(mesh):
    return jax.shard_map(
        shards,
        mesh=mesh,
        in_specs=(P(("row", "col"), None), P(("row", "col")), P()),
        out_specs=P(None, ("row", "col")),
        check_vma=False,
    )
```
